32 devices in a mesh: seq: 8 (over z, y), ch: 4 (over x, core).
Axes of the slice: x: 2, y: 2, z: 4, core: 2. Of those that a mesh axis runs over, the one named last changes fastest.
Arguments:
- tokens: bfloat16 [32768, 1024], P('seq', 'ch'), may hold values from -6 to 6
- cotangent: bfloat16 [32768, 1024], P('seq', 'ch'), may hold values from -6 to 6
- first_factor: bfloat16 [16, 64, 64], replicated, may hold values from -0.75 to 0.75
- second_factor: bfloat16 [64, 16, 16], replicated, may hold values from -1.5 to 1.5
- third_factor: bfloat16 [64, 32, 32], replicated, may hold values from -1 to 1
- gate_weight: bfloat16 [1024, 1024], P(None, 'ch'), may hold values from -0.1875 to 0.1875
Outputs:
- output: bfloat16 [32768, 1024], P('seq', 'ch')
- input_grad: bfloat16 [32768, 1024], P('seq', 'ch')
- first_grad: bfloat16 [16, 64, 64], replicated
- second_grad: bfloat16 [64, 16, 16], replicated
- third_grad: bfloat16 [64, 32, 32], replicated
- gate_grad: float32 [1024, 1024], P('seq', 'ch')
The draws below stay inside these ranges and needn't reach their ends.
All inputs are finite; a program needn't handle non-finite values.
Results may differ from the reference program's by a relative error of at most 0.0068.
Values may be sent and summed in bfloat16 or wider, within the bound.
No kernel may reach another device: no remote copies, remote signals or barrier semaphores. Data moves between devices by JAX's collectives and lax.ppermute only.
A program may use at most 64 MiB of HBM per device.

```python
import jax
import jax.numpy as jnp

A = 32
B = 16
C = 64
D = 1024
L = 32768


def spiked(result, stream_key, source, target, blocks, factor):
    def block_of(axis_at):
        return (jnp.arange(result.shape[axis_at]) // (result.shape[axis_at] // blocks)).reshape((-1,) + (1,) * (result.ndim - 1 - axis_at))

    near = jax.random.permutation(stream_key, blocks)[block_of(target)]
    second = (block_of(target) + blocks // 2) % blocks
    return jnp.where((block_of(source) == near) | (block_of(source) == second), factor * result, result)


def levels(rng, shape, split, low, top_value):
    loudness, own = 1.0, jax.random.fold_in(rng, 6)
    for position, parts in split:
        draws = jnp.exp(jax.random.uniform(jax.random.fold_in(own, position), (parts,), jnp.float32, low / len(split), top_value / len(split)))
        loudness = loudness * jnp.repeat(draws, shape[position] // parts).reshape([-1 if axis == position else 1 for axis in range(len(shape))])
    return loudness


def noise(own_key, extent, width, most, shards=(), held_as=jnp.bfloat16):
    array = width * jax.random.normal(own_key, extent, jnp.float32)
    if shards:
        array = array * levels(own_key, extent, shards, -0.22, 0.18)
    return jnp.clip(array, -most, most).astype(held_as)


def gaussian_with(stream_key, dims, deviation, limit, shards, heavy, held_as=jnp.bfloat16):
    entries = deviation * jax.random.normal(stream_key, dims, jnp.float32)
    if shards:
        entries = entries * levels(stream_key, dims, shards, -0.22, 0.18)
    return jnp.clip(spiked(entries, jax.random.fold_in(stream_key, 3), *heavy), -limit, limit).astype(held_as)


def setup_inputs(seed: int = 0) -> dict:
    splits = jax.random.split(jax.random.key(seed), 7)
    return {
        "tokens": gaussian_with(splits[0], (L, D), 1.0, 6.0, ((0, 8), (1, 4)), (0, 1, 8, 2.0)),
        "cotangent": noise(splits[1], (L, D), 1.0, 6.0, ((0, 8), (1, 4))),
        "first_factor": noise(splits[2], (B, C, C), C ** -0.5, 0.75),
        "second_factor": noise(splits[3], (C, B, B), B ** -0.5, 1.5),
        "third_factor": noise(splits[4], (C, A, A), A ** -0.5, 1.0),
        "gate_weight": noise(splits[5], (D, D), D ** -0.5, 0.1875, ((1, 4),)),
    }


def reference(tokens, cotangent, first_factor, second_factor, third_factor, gate_weight):
    grid_in = tokens.reshape(A, B, C, D).astype(jnp.float32)
    first_w = first_factor.astype(jnp.float32)
    second_w = second_factor.astype(jnp.float32)
    third_w = third_factor.astype(jnp.float32)
    mixed_first = jnp.einsum("bcd,abdh->abch", first_w, grid_in).astype(jnp.bfloat16)
    mixed_second = jnp.einsum("cbe,aech->abch", second_w, mixed_first.astype(jnp.float32)).astype(jnp.bfloat16)
    mixed = jnp.einsum("cae,ebch->abch", third_w, mixed_second.astype(jnp.float32)).astype(jnp.bfloat16)
    mixed_flat = mixed.reshape(L, D).astype(jnp.float32)
    gate_pre = jnp.dot(tokens, gate_weight, preferred_element_type=jnp.float32)
    sigmoid_gate = jax.nn.sigmoid(gate_pre)
    activation = gate_pre * sigmoid_gate
    output = (tokens.astype(jnp.float32) + mixed_flat * activation).astype(jnp.bfloat16)
    upstream = cotangent.astype(jnp.float32)
    mix_grad = (upstream * activation).astype(jnp.bfloat16)
    pre_grad = (upstream * mixed_flat * sigmoid_gate * (1.0 + gate_pre * (1.0 - sigmoid_gate))).astype(jnp.bfloat16)
    grad_grid = mix_grad.reshape(A, B, C, D).astype(jnp.float32)
    back_second = jnp.einsum("cae,abch->ebch", third_w, grad_grid).astype(jnp.bfloat16)
    third_grad = jnp.einsum("abch,ebch->cae", grad_grid, mixed_second.astype(jnp.float32))
    back_first = jnp.einsum("cbe,abch->aech", second_w, back_second.astype(jnp.float32)).astype(jnp.bfloat16)
    second_grad = jnp.einsum("abch,aech->cbe", back_second.astype(jnp.float32), mixed_first.astype(jnp.float32))
    mix_input = jnp.einsum("bcd,abch->abdh", first_w, back_first.astype(jnp.float32)).reshape(L, D)
    first_grad = jnp.einsum("abch,abdh->bcd", back_first.astype(jnp.float32), grid_in)
    gate_input = jnp.dot(pre_grad, gate_weight.T, preferred_element_type=jnp.float32)
    gate_grad = jnp.dot(tokens.T, pre_grad, preferred_element_type=jnp.float32)
    input_grad = (upstream + mix_input + gate_input).astype(jnp.bfloat16)
    return (output, input_grad, first_grad.astype(jnp.bfloat16), second_grad.astype(jnp.bfloat16),
            third_grad.astype(jnp.bfloat16), gate_grad)
```

```python
import functools

import jax
import jax.numpy as jnp
from jax import lax
from jax.experimental import pallas as pl
from jax.experimental.pallas import tpu as pltpu
from jax.sharding import PartitionSpec as P

A = 32
B = 16
C = 64
PER = 8
F32 = jnp.float32
BF16 = jnp.bfloat16
VMEM_BYTES = 56 * 1024 * 1024


def swap(values, axis, step):
    count = lax.axis_size(axis)
    return lax.ppermute(values, axis, [(i, i ^ step) for i in range(count)])


def flip_blocks(values, dim, index):
    count = values.shape[dim]
    bit = 1
    while bit < count:
        shape = values.shape[:dim] + (count // (2 * bit), 2, bit) + values.shape[dim + 1 :]
        split = values.reshape(shape)
        turned = jnp.flip(split, dim + 1)
        values = jnp.where((index // bit) % 2 == 1, turned, split).reshape(values.shape)
        bit *= 2
    return values


def exchange(pieces):
    moved = {j: swap(pieces[j], "seq", j) for j in range(len(pieces) - 1, 0, -1)}
    return [pieces[0]] + [moved[j] for j in range(1, len(pieces))]


def dot(left, right, dims=((1,), (0,))):
    return lax.dot_general(left, right, (dims, ((), ())), preferred_element_type=F32)


def rows_of(block, count):
    return pl.ds(pl.multiple_of(block * count, count), count)


def call(kernel, grid, index, ins, in_specs, outs, out_specs, scratch=(), flops=0, name=None):
    moved = sum(x.size * x.dtype.itemsize for x in list(ins) + list(outs))
    return pl.pallas_call(
        kernel,
        grid_spec=pltpu.PrefetchScalarGridSpec(
            num_scalar_prefetch=1,
            grid=grid,
            in_specs=in_specs,
            out_specs=out_specs,
            scratch_shapes=scratch,
        ),
        out_shape=outs,
        compiler_params=pltpu.CompilerParams(
            dimension_semantics=("arbitrary",) * len(grid), vmem_limit_bytes=VMEM_BYTES
        ),
        cost_estimate=pl.CostEstimate(flops=flops, transcendentals=0, bytes_accessed=moved),
        name=name,
    )(index, *ins)


def shape(dims, dtype):
    return jax.ShapeDtypeStruct(dims, dtype)


def whole(x):
    dims = x.shape
    return pl.BlockSpec(dims, lambda *_: (0,) * len(dims))


def by_row(x, parts):
    dims = (x.shape[0] // parts,) + tuple(x.shape[1:])
    return pl.BlockSpec(dims, lambda i, *_: (i,) + (0,) * (len(dims) - 1))


def scatter_rows(source, pieces, me, pair):
    for j, piece in enumerate(pieces):
        low = source[0, rows_of(me ^ j, PER), :]
        high = source[1, rows_of(me ^ j, PER), :]
        piece[0, pair] = jnp.concatenate([low, high], 0).astype(BF16)


def gather_rows(target, pieces, me, pair):
    for j, piece in enumerate(pieces):
        both = piece[0, pair].astype(F32)
        target[0, rows_of(me ^ j, PER), :] = both[:PER]
        target[1, rows_of(me ^ j, PER), :] = both[PER:]


def first_kernel(index, tokens, factor, *rest):
    pieces, held = rest[:-1], rest[-1]
    for pair in range(B // 2):
        for side in range(2):
            b = 2 * pair + side
            held[pair % 2, side] = dot(factor[b], tokens[b * C : (b + 1) * C, :])
        scatter_rows(held.at[pair % 2], pieces, index[0], pair)


def far_kernel(n, own_a, index, *refs):
    first, (second_big, third_big), second_out, pieces = (
        refs[:n], refs[n : n + 2], refs[n + 2], refs[n + 3 :]
    )
    for j in range(n):
        for i in range(own_a):
            block = first[j][i].reshape(B * PER, -1)
            mixed = dot(second_big[...], block).astype(BF16)
            second_out[j * own_a + i] = mixed.reshape(second_out.shape[1:])
    for pair in range(B // 2):
        block = second_out[:, pair].reshape(2 * A * PER, -1)
        mixed = dot(third_big[...], block).astype(BF16).reshape(A, 2 * PER, -1)
        for j in range(n):
            pieces[j][:, pair] = mixed[j * own_a : (j + 1) * own_a]


def gate_kernel(m, index, *refs):
    gathered, (weight, upstream, gate_out), pieces, held = (
        refs[:m], refs[m : m + 3], refs[m + 3 : -1], refs[-1]
    )
    width = weight.shape[1]
    for pair in range(B // 2):
        rows = slice(pair * 2 * C, (pair + 1) * 2 * C)
        gate = 0.0
        for j in range(m):
            gate += dot(gathered[j][rows, :], weight[rows_of(index[1] ^ j, width), :])
        gate_out[rows, :] = gate
        grad = upstream[rows, :].astype(F32) * (gate * jax.nn.sigmoid(gate))
        held[pair % 2] = grad.reshape(2, C, width)
        scatter_rows(held.at[pair % 2], pieces, index[0], pair)


def output_kernel(n, index, *refs):
    pieces, (gate_in, tokens, upstream, output, pre_grad, held) = refs[:n], refs[n:]
    for pair in range(B // 2):
        rows = slice(pair * 2 * C, (pair + 1) * 2 * C)
        gather_rows(held.at[pair % 2], pieces, index[0], pair)
        mixed = held[pair % 2].reshape(2 * C, -1)
        gate = gate_in[rows, :]
        sig = jax.nn.sigmoid(gate)
        output[rows, :] = (tokens[rows, :].astype(F32) + mixed * (gate * sig)).astype(BF16)
        pre_grad[rows, :] = (
            upstream[rows, :].astype(F32) * mixed * sig * (1.0 + gate * (1.0 - sig))
        ).astype(BF16)


def split_dot(values, selector):
    top = values.astype(BF16)
    rest = values - top.astype(F32)
    middle = rest.astype(BF16)
    low = (rest - middle.astype(F32)).astype(BF16)
    return dot(top, selector) + dot(middle, selector) + dot(low, selector)


def back_kernel(n, own_a, index, *refs):
    grads, first = refs[:n], refs[n : 2 * n]
    second_val, second_big, third_big, sums = refs[2 * n : 2 * n + 4]
    pieces, (back_second, third_acc, second_acc) = refs[2 * n + 4 : -3], refs[-3:]
    big = 2 * A * PER
    small = B * PER
    for pair in range(B // 2):
        block = jnp.concatenate([g[:, pair].reshape(own_a * 2 * PER, -1) for g in grads], 0)
        back = dot(third_big[...], block).astype(BF16)
        back_second[:, pair] = back.reshape(A, 2 * PER, -1)
        part = dot(block, second_val[:, pair].reshape(big, -1), ((1,), (1,)))
        third_acc[...] = part if pair == 0 else third_acc[...] + part
    for j in range(n):
        for i in range(own_a):
            block = back_second[j * own_a + i].reshape(small, -1)
            pieces[j][i] = dot(second_big[...], block).astype(BF16).reshape(pieces[j].shape[1:])
            part = dot(block, first[j][i].reshape(small, -1), ((1,), (1,)))
            second_acc[...] = part if j + i == 0 else second_acc[...] + part
    row = lax.broadcasted_iota(jnp.int32, (128, big), 0)
    col = lax.broadcasted_iota(jnp.int32, (128, big), 1)
    keep = row % (2 * PER) == col % (2 * PER)
    expand = lax.broadcasted_iota(jnp.int32, (big, 128), 0) // (2 * PER)
    lane = lax.broadcasted_iota(jnp.int32, (big, 128), 1)
    total = 0.0
    for g in range(big // 128):
        picked = jnp.where(keep, third_acc[g * 128 : (g + 1) * 128, :], 0.0)
        total += split_dot(picked, (lane == expand + g * A).astype(BF16))
    total = total.reshape(128 // (2 * PER), 2, PER, 128)
    sums[0 : 128 // 2, :] = (total[:, 0] + total[:, 1]).reshape(128 // 2, 128)
    row = lax.broadcasted_iota(jnp.int32, (2 * PER, small), 0)
    col = lax.broadcasted_iota(jnp.int32, (2 * PER, small), 1)
    keep = row % PER == col % PER
    expand = lax.broadcasted_iota(jnp.int32, (small, 128), 0) // PER
    lane = lax.broadcasted_iota(jnp.int32, (small, 128), 1)
    total = 0.0
    for g in range(small // (2 * PER)):
        picked = jnp.where(keep, second_acc[g * 2 * PER : (g + 1) * 2 * PER, :], 0.0)
        total += split_dot(picked, (lane == expand + g * B).astype(BF16))
    sums[128 // 2 :, :] = total


def gate_grad_kernel(m, index, *refs):
    gathered, pre_grad, out = refs[:m], refs[m], refs[m + 1]
    width = pre_grad.shape[1]

    @pl.when(pl.program_id(0) == 0)
    def _():
        out[...] = jnp.zeros_like(out)

    for j in range(m):
        out[rows_of(index[1] ^ j, width), :] += dot(
            gathered[j][...], pre_grad[...], ((0,), (0,))
        )


def gate_input_kernel(m, index, *refs):
    grads, weights, upstream, out = refs[:m], refs[m : 2 * m], refs[2 * m], refs[2 * m + 1]
    total = upstream[...].astype(F32)
    for j in range(m):
        total += dot(grads[j][...], weights[j][...], ((1,), (1,)))
    out[...] = total


def first_grad_kernel(n, index, *refs):
    pieces, (tokens, back, out, held) = refs[:n], refs[n:]

    @pl.when(pl.program_id(0) == 0)
    def _():
        out[...] = jnp.zeros_like(out)

    for pair in range(B // 2):
        gather_rows(held.at[pair % 2], pieces, index[0], pair)
        sides = []
        for side in range(2):
            rows = slice((2 * pair + side) * C, (2 * pair + side + 1) * C)
            value = held[pair % 2, side].astype(BF16)
            back[rows, :] = value
            sides.append(dot(value, tokens[rows, :], ((1,), (1,))))
        both = jnp.concatenate(sides, 1).reshape(C // PER, PER, 2 * C)
        out[:, pair] += both


def input_grad_kernel(index, back, factor, partial, out):
    for b in range(B):
        rows = slice(b * C, (b + 1) * C)
        mixed = dot(factor[b], back[rows, :], ((0,), (0,)))
        out[rows, :] = (partial[rows, :] + mixed).astype(BF16)


def spread_diagonal(values, copies):
    rows, c, cols = values.shape
    tall = jnp.broadcast_to(values[:, None], (rows, copies, c, cols))
    tall = tall.reshape(rows * copies * c, cols)
    wide = cols * copies * c
    expand = (
        lax.broadcasted_iota(jnp.int32, (cols, wide), 1) // (copies * c)
        == lax.broadcasted_iota(jnp.int32, (cols, wide), 0)
    ).astype(BF16)
    dims = (tall.shape[0], wide)
    keep = (
        lax.broadcasted_iota(jnp.int32, dims, 0) % (copies * c)
        == lax.broadcasted_iota(jnp.int32, dims, 1) % (copies * c)
    )
    return jnp.where(keep, dot(tall, expand), 0.0).astype(BF16)


def resident(tokens, cotangent, first_factor, second_factor, third_factor, gate_weight):
    n = lax.axis_size("seq")
    s = lax.axis_index("seq")
    m = lax.axis_size("ch")
    q = lax.axis_index("ch")
    rows, width = tokens.shape
    own_a = rows // (B * C)
    index = jnp.stack([s, q]).astype(jnp.int32)
    piece = shape((own_a, B // 2, 2 * PER, width), BF16)
    piece_rows = [by_row(piece, own_a)] * n
    row_blocks = by_row(tokens, own_a)
    pair_rows = pltpu.VMEM((2, 2, C, width), F32)

    far_tokens = swap(tokens, "ch", 2)
    sent = call(
        first_kernel, (own_a,), index, (tokens, first_factor),
        [row_blocks, whole(first_factor)], [piece] * n, piece_rows, [pair_rows],
        2 * rows * width * C, "first_mix",
    )
    first_far = exchange(sent)
    gathered = [tokens, swap(tokens, "ch", 1), far_tokens, swap(far_tokens, "ch", 1)]
    weight_rows = [
        lax.dynamic_slice_in_dim(gate_weight, (q ^ j) * width, width, 0) for j in range(m)
    ]
    back_weight = [weight_rows[0]] + [swap(weight_rows[j], "ch", j) for j in range(1, m)]

    second_own = lax.dynamic_slice_in_dim(second_factor, s * PER, PER, 0)
    third_own = lax.dynamic_slice_in_dim(third_factor, s * PER, PER, 0)
    third_own = third_own.reshape(PER, n, own_a, n, own_a)
    third_own = flip_blocks(flip_blocks(third_own, 1, s), 3, s).reshape(PER, A, A)
    second_big = spread_diagonal(second_own.transpose(1, 0, 2), 1)
    second_back = spread_diagonal(second_own.transpose(2, 0, 1), 1)
    third_big = spread_diagonal(third_own.transpose(1, 0, 2), 2)
    third_back = spread_diagonal(third_own.transpose(2, 0, 1), 2)

    far = shape((A, B // 2, 2 * PER, width), BF16)
    ins = (*first_far, second_big, third_big)
    outs = [far] + [piece] * n
    second_far, *sent = call(
        functools.partial(far_kernel, n, own_a), (1,), index, ins,
        [whole(x) for x in ins], outs, [whole(x) for x in outs],
        (), 2 * rows * width * 6 * C, "far_mix",
    )
    mixed_home = exchange(sent)

    gate_shape = shape((rows, width), F32)
    ins = (*gathered, gate_weight, cotangent)
    gate_pre, *sent = call(
        functools.partial(gate_kernel, m), (own_a,), index, ins,
        [row_blocks] * m + [whole(gate_weight), row_blocks],
        [gate_shape] + [piece] * n, [row_blocks] + piece_rows, [pair_rows],
        2 * rows * width * m * width, "gate",
    )
    grad_far = exchange(sent)

    ins = (*mixed_home, gate_pre, tokens, cotangent)
    output, pre_grad = call(
        functools.partial(output_kernel, n), (own_a,), index, ins,
        piece_rows + [row_blocks] * 3, [shape((rows, width), BF16)] * 2, [row_blocks] * 2,
        [pair_rows], rows * width * 16, "output",
    )
    far_pre = swap(pre_grad, "ch", 2)
    all_pre = [pre_grad, swap(pre_grad, "ch", 1), far_pre, swap(far_pre, "ch", 1)]

    ins = (*grad_far, *first_far, second_far, second_back, third_back)
    outs = [shape((128 // 2 + 2 * PER, 128), F32)] + [piece] * n
    sums, *sent = call(
        functools.partial(back_kernel, n, own_a), (1,), index, ins,
        [whole(x) for x in ins], outs, [whole(x) for x in outs],
        [
            pltpu.VMEM(far.shape, BF16),
            pltpu.VMEM((2 * A * PER, 2 * A * PER), F32),
            pltpu.VMEM((B * PER, B * PER), F32),
        ],
        2 * rows * width * 16 * C, "far_back",
    )
    back_home = exchange(sent)

    out = shape((m * width, width), F32)
    gate_part = call(
        functools.partial(gate_grad_kernel, m), (own_a,), index, (*gathered, pre_grad),
        [row_blocks] * (m + 1), [out], [whole(out)], (),
        2 * rows * width * m * width, "gate_grad",
    )[0].reshape(n, m * width // n, width)
    bit = 1
    while bit < n:
        mine = (s // bit) % 2
        split = gate_part.reshape(n // (2 * bit), 2, *gate_part.shape[1:])
        keep = lax.dynamic_index_in_dim(split, mine, 1, False)
        send = lax.dynamic_index_in_dim(split, 1 - mine, 1, False)
        gate_part = keep + swap(send, "seq", bit)
        bit *= 2
    gate_grad = gate_part.reshape(m * width // n, width)

    ins = (*all_pre, *back_weight, cotangent)
    partial = call(
        functools.partial(gate_input_kernel, m), (own_a,), index, ins,
        [row_blocks] * m + [whole(w) for w in back_weight] + [row_blocks],
        [gate_shape], [row_blocks], (), 2 * rows * width * m * width, "gate_input",
    )[0]

    bit = m // 2
    while bit:
        sums = sums + swap(sums, "ch", bit)
        bit //= 2
    every = sums.astype(BF16)[None]
    bit = 1
    while bit < n:
        other = swap(every, "seq", bit)
        every = jnp.where(
            (s // bit) % 2 == 1,
            jnp.concatenate([other, every], 0),
            jnp.concatenate([every, other], 0),
        )
        bit *= 2
    third_all = every[:, : 128 // 2].reshape(n, A // 4, PER, 4, A)
    third_all = third_all.transpose(0, 2, 3, 1, 4).reshape(n, PER, n, own_a, n, own_a)
    owner = jnp.arange(n)
    place = (owner[:, None] ^ owner[None, :]).astype(jnp.int32)
    third_grad = jnp.stack(
        [third_all[o][:, place[o]][:, :, :, place[o]] for o in range(n)]
    ).reshape(C, A, A)
    second_all = every[:, 128 // 2 :].reshape(n, 2, PER, B // 2, B)
    second_grad = second_all.transpose(0, 2, 3, 1, 4).reshape(C, B, B)

    ins = (*back_home, tokens)
    first_out = shape((n, B // 2, PER, 2 * C), F32)
    back_rows, first_part = call(
        functools.partial(first_grad_kernel, n), (own_a,), index, ins,
        piece_rows + [row_blocks], [shape((rows, width), BF16), first_out],
        [row_blocks, whole(first_out)], [pair_rows], 2 * rows * width * C, "first_grad",
    )
    parts = first_part.reshape(n * m, -1, 128)
    parts = lax.all_to_all(parts, ("seq", "ch"), split_axis=0, concat_axis=0, tiled=True)
    first_sum = parts.sum(0).astype(BF16)
    first_sum = lax.all_to_all(
        jnp.broadcast_to(first_sum[None], (n * m, *first_sum.shape)),
        ("seq", "ch"), split_axis=0, concat_axis=0, tiled=True,
    )
    first_grad = first_sum.reshape(n, B // 2, PER, 2, C).transpose(1, 3, 0, 2, 4)
    first_grad = first_grad.reshape(B, C, C)

    ins = (back_rows, first_factor, partial)
    input_grad = call(
        input_grad_kernel, (own_a,), index, ins,
        [row_blocks, whole(first_factor), row_blocks],
        [shape((rows, width), BF16)], [row_blocks], (), 2 * rows * width * C, "input_grad",
    )[0]
    return output, input_grad, first_grad, second_grad, third_grad, gate_grad


def spread_out(tokens, cotangent, first_factor, second_factor, third_factor, gate_weight):
    seq_count = lax.axis_size("seq")
    seq_index = lax.axis_index("seq")
    per_device_c = max(1, C // seq_count)
    splits = max(1, seq_count // C)
    local_rows, width = tokens.shape
    narrow = width // splits
    blocks = local_rows // C
    batch_b = min(blocks, B)
    start_b = seq_index * blocks % B
    if blocks >= B:
        first_sel = first_factor
    else:
        first_sel = lax.dynamic_slice_in_dim(first_factor, start_b, blocks, 0)
    column = seq_index // splits * per_device_c
    second_sel = lax.dynamic_slice_in_dim(second_factor, column, per_device_c, 0)
    third_sel = lax.dynamic_slice_in_dim(third_factor, column, per_device_c, 0)
    grid_view = tokens.reshape(blocks // batch_b, batch_b, C, width)
    mixed_first = jnp.einsum(
        "bcd,ibdh->ibch", first_sel, grid_view, preferred_element_type=jnp.float32
    ).astype(jnp.bfloat16)

    def spread(values):
        return values.reshape(blocks, seq_count, per_device_c, narrow)

    received = lax.all_to_all(spread(mixed_first), "seq", split_axis=1, concat_axis=0, tiled=True)
    item_count = received.shape[3]
    far_view = received.reshape(A, B, per_device_c, item_count)
    second_val = jnp.einsum(
        "kbe,aekh->abkh", second_sel, far_view, preferred_element_type=jnp.float32
    ).astype(jnp.bfloat16)
    third_val = jnp.einsum(
        "kae,ebkh->abkh", third_sel, second_val, preferred_element_type=jnp.float32
    ).astype(jnp.bfloat16)
    first_far = received
    second_far = second_val.reshape(A * B, 1, per_device_c, item_count)
    mixed_far = third_val.reshape(A * B, 1, per_device_c, item_count)
    mixed_back = lax.all_to_all(mixed_far, "seq", split_axis=0, concat_axis=1, tiled=True).reshape(
        local_rows, width
    )
    full_tokens, full_weight = (
        lax.all_gather(tokens, "ch", axis=1, tiled=True),
        lax.all_gather(gate_weight, "ch", axis=1, tiled=True),
    )
    own_rows = lax.dynamic_slice_in_dim(full_weight, lax.axis_index("ch") * width, width, 0)
    gate_pre = jnp.dot(full_tokens, gate_weight, preferred_element_type=jnp.float32)
    sigmoid_gate = jax.nn.sigmoid(gate_pre)
    activation = gate_pre * sigmoid_gate
    mixed_float = mixed_back.astype(jnp.float32)
    output = (tokens.astype(jnp.float32) + mixed_float * activation).astype(jnp.bfloat16)
    upstream = cotangent.astype(jnp.float32)
    mix_grad = (upstream * activation).astype(jnp.bfloat16)
    pre_grad = (
        upstream * mixed_float * sigmoid_gate * (1.0 + gate_pre * (1.0 - sigmoid_gate))
    ).astype(jnp.bfloat16)
    received = lax.all_to_all(spread(mix_grad), "seq", split_axis=1, concat_axis=0, tiled=True)
    item_count = received.shape[3]
    far_view = received.reshape(A, B, per_device_c, item_count)
    back_second = jnp.einsum(
        "kae,abkh->ebkh", third_sel, far_view, preferred_element_type=jnp.float32
    ).astype(jnp.bfloat16)
    back_first = jnp.einsum(
        "kbe,abkh->aekh", second_sel, back_second, preferred_element_type=jnp.float32
    ).astype(jnp.bfloat16)
    second_back = back_second.reshape(A * B, 1, per_device_c, item_count)
    first_back = back_first.reshape(A * B, 1, per_device_c, item_count)
    third_part = jnp.einsum(
        "abkh,ebkh->kae",
        received.reshape(A, B, per_device_c, narrow),
        second_far.reshape(A, B, per_device_c, narrow),
        preferred_element_type=jnp.float32,
    )
    second_part = jnp.einsum(
        "abkh,aekh->kbe",
        second_back.reshape(A, B, per_device_c, narrow),
        first_far.reshape(A, B, per_device_c, narrow),
        preferred_element_type=jnp.float32,
    )
    first_home = lax.all_to_all(first_back, "seq", split_axis=0, concat_axis=1, tiled=True).reshape(
        blocks // batch_b, batch_b, C, width
    )
    mix_input = jnp.einsum(
        "bcd,ibch->ibdh", first_sel, first_home, preferred_element_type=jnp.float32
    ).reshape(local_rows, width)
    first_part = jnp.einsum(
        "ibch,ibdh->bcd", first_home, grid_view, preferred_element_type=jnp.float32
    )
    if blocks >= B:
        first_full = first_part
    else:
        first_full = lax.dynamic_update_slice_in_dim(
            jnp.zeros((B, C, C), jnp.float32), first_part, start_b, 0
        )
    second_full = lax.dynamic_update_slice_in_dim(
        jnp.zeros((C, B, B), jnp.float32), second_part, column, 0
    )
    third_full = lax.dynamic_update_slice_in_dim(
        jnp.zeros((C, A, A), jnp.float32), third_part, column, 0
    )
    first_sum, second_sum, third_sum = lax.psum(
        (first_full, second_full, third_full), ("seq", "ch")
    )
    gate_input = lax.dot_general(
        lax.all_gather(pre_grad, "ch", axis=1, tiled=True),
        own_rows,
        (((1,), (1,)), ((), ())),
        preferred_element_type=jnp.float32,
    )
    gate_grad = lax.psum_scatter(
        lax.dot_general(
            full_tokens, pre_grad, (((0,), (0,)), ((), ())), preferred_element_type=jnp.float32
        ),
        "seq",
        scatter_dimension=0,
        tiled=True,
    )
    input_grad = (upstream + mix_input + gate_input).astype(jnp.bfloat16)
    return (
        output,
        input_grad,
        first_sum.astype(jnp.bfloat16),
        second_sum.astype(jnp.bfloat16),
        third_sum.astype(jnp.bfloat16),
        gate_grad,
    )


def on_device(*arrays):
    n = lax.axis_size("seq")
    rows = arrays[0].shape[0]
    square = lax.axis_size("ch") == 4 and n * PER == C
    if square and rows % (B * C) == 0 and rows * n == A * B * C:
        return resident(*arrays)
    return spread_out(*arrays)


def solution(mesh):
    placed = (P("seq", "ch"), P("seq", "ch"), P(), P(), P(), P(None, "ch"))
    return jax.shard_map(
        on_device,
        mesh=mesh,
        in_specs=placed,
        out_specs=(P("seq", "ch"), P("seq", "ch"), P(), P(), P(), P("seq", "ch")),
        check_vma=False,
    )
```

```python
import functools

import jax
import jax.numpy as jnp
from jax import lax
from jax.experimental import pallas as pl
from jax.experimental.pallas import tpu as pltpu
from jax.sharding import PartitionSpec as P

A = 32
B = 16
C = 64
PER = 8
F32 = jnp.float32
BF16 = jnp.bfloat16
VMEM_BYTES = 56 * 1024 * 1024


def swap(values, axis, step):
    count = lax.axis_size(axis)
    return lax.ppermute(values, axis, [(i, i ^ step) for i in range(count)])


def flip_blocks(values, dim, index):
    count = values.shape[dim]
    bit = 1
    while bit < count:
        shape = values.shape[:dim] + (count // (2 * bit), 2, bit) + values.shape[dim + 1 :]
        split = values.reshape(shape)
        turned = jnp.flip(split, dim + 1)
        values = jnp.where((index // bit) % 2 == 1, turned, split).reshape(values.shape)
        bit *= 2
    return values


def exchange(pieces):
    moved = {}
    for j in range(len(pieces) - 1, 0, -1):
        moved[j] = swap(pieces[j], "seq", j)
    return [pieces[0]] + [moved[j] for j in range(1, len(pieces))]


def dot(left, right, dims=((1,), (0,))):
    return lax.dot_general(left, right, (dims, ((), ())), preferred_element_type=F32)


def rows_of(block, count):
    return pl.ds(pl.multiple_of(block * count, count), count)


def call(kernel, grid, index, ins, in_specs, outs, out_specs, scratch=(), flops=0):
    moved = sum(x.size * x.dtype.itemsize for x in list(ins) + list(outs))
    return pl.pallas_call(
        kernel,
        grid_spec=pltpu.PrefetchScalarGridSpec(
            num_scalar_prefetch=1,
            grid=grid,
            in_specs=in_specs,
            out_specs=out_specs,
            scratch_shapes=scratch,
        ),
        out_shape=outs,
        compiler_params=pltpu.CompilerParams(
            dimension_semantics=("arbitrary",) * len(grid), vmem_limit_bytes=VMEM_BYTES
        ),
        cost_estimate=pl.CostEstimate(flops=flops, transcendentals=0, bytes_accessed=moved),
    )(index, *ins)


def shape(dims, dtype):
    return jax.ShapeDtypeStruct(dims, dtype)


def whole(x):
    dims = x.shape
    return pl.BlockSpec(dims, lambda *_: (0,) * len(dims))


def by_row(x, parts):
    dims = (x.shape[0] // parts,) + tuple(x.shape[1:])
    return pl.BlockSpec(dims, lambda i, *_: (i,) + (0,) * (len(dims) - 1))


def scatter_rows(source, pieces, me, pair):
    for j, piece in enumerate(pieces):
        low = source[0, rows_of(me ^ j, PER), :]
        high = source[1, rows_of(me ^ j, PER), :]
        piece[0, pair] = jnp.concatenate([low, high], 0).astype(BF16)


def gather_rows(target, pieces, me, pair):
    for j, piece in enumerate(pieces):
        both = piece[0, pair].astype(F32)
        target[0, rows_of(me ^ j, PER), :] = both[:PER]
        target[1, rows_of(me ^ j, PER), :] = both[PER:]


def first_kernel(index, tokens, factor, *rest):
    pieces, held = rest[:-1], rest[-1]
    for pair in range(B // 2):
        for side in range(2):
            b = 2 * pair + side
            held[pair % 2, side] = dot(factor[b], tokens[b * C : (b + 1) * C, :])
        scatter_rows(held.at[pair % 2], pieces, index[0], pair)


def far_kernel(n, own_a, index, *refs):
    first, (second_big, third_big), second_out, pieces = (
        refs[:n], refs[n : n + 2], refs[n + 2], refs[n + 3 :]
    )
    for j in range(n):
        for i in range(own_a):
            block = first[j][i].reshape(B * PER, -1)
            mixed = dot(second_big[...], block).astype(BF16)
            second_out[j * own_a + i] = mixed.reshape(second_out.shape[1:])
    for pair in range(B // 2):
        block = second_out[:, pair].reshape(2 * A * PER, -1)
        mixed = dot(third_big[...], block).astype(BF16).reshape(A, 2 * PER, -1)
        for j in range(n):
            pieces[j][:, pair] = mixed[j * own_a : (j + 1) * own_a]


def gate_kernel(m, index, *refs):
    gathered, (weight, upstream, gate_out), pieces, held = (
        refs[:m], refs[m : m + 3], refs[m + 3 : -1], refs[-1]
    )
    width = weight.shape[1]
    for pair in range(B // 2):
        rows = slice(pair * 2 * C, (pair + 1) * 2 * C)
        gate = 0.0
        for j in range(m):
            gate += dot(gathered[j][rows, :], weight[rows_of(index[1] ^ j, width), :])
        gate_out[rows, :] = gate
        grad = upstream[rows, :].astype(F32) * (gate * jax.nn.sigmoid(gate))
        held[pair % 2] = grad.reshape(2, C, width)
        scatter_rows(held.at[pair % 2], pieces, index[0], pair)


def output_kernel(n, index, *refs):
    pieces, (gate_in, tokens, upstream, output, pre_grad, held) = refs[:n], refs[n:]
    for pair in range(B // 2):
        rows = slice(pair * 2 * C, (pair + 1) * 2 * C)
        gather_rows(held.at[pair % 2], pieces, index[0], pair)
        mixed = held[pair % 2].reshape(2 * C, -1)
        gate = gate_in[rows, :]
        sig = jax.nn.sigmoid(gate)
        output[rows, :] = (tokens[rows, :].astype(F32) + mixed * (gate * sig)).astype(BF16)
        pre_grad[rows, :] = (
            upstream[rows, :].astype(F32) * mixed * sig * (1.0 + gate * (1.0 - sig))
        ).astype(BF16)


def split_dot(values, selector):
    top = values.astype(BF16)
    rest = values - top.astype(F32)
    middle = rest.astype(BF16)
    low = (rest - middle.astype(F32)).astype(BF16)
    return dot(top, selector) + dot(middle, selector) + dot(low, selector)


def back_kernel(n, own_a, index, *refs):
    grads, (second_big, third_big, back_second), pieces = refs[:n], refs[n : n + 3], refs[n + 3 :]
    for pair in range(B // 2):
        block = jnp.concatenate([g[:, pair].reshape(own_a * 2 * PER, -1) for g in grads], 0)
        back = dot(third_big[...], block).astype(BF16)
        back_second[:, pair] = back.reshape(A, 2 * PER, -1)
    for j in range(n):
        for i in range(own_a):
            block = back_second[j * own_a + i].reshape(B * PER, -1)
            pieces[j][i] = dot(second_big[...], block).astype(BF16).reshape(pieces[j].shape[1:])


def far_grad_kernel(n, own_a, index, *refs):
    grads, first = refs[:n], refs[n : 2 * n]
    second_val, back_second, sums, third_acc, second_acc = refs[2 * n :]
    big = 2 * A * PER
    small = B * PER
    for pair in range(B // 2):
        block = jnp.concatenate([g[:, pair].reshape(own_a * 2 * PER, -1) for g in grads], 0)
        part = dot(block, second_val[:, pair].reshape(big, -1), ((1,), (1,)))
        third_acc[...] = part if pair == 0 else third_acc[...] + part
    for j in range(n):
        for i in range(own_a):
            block = back_second[j * own_a + i].reshape(small, -1)
            part = dot(block, first[j][i].reshape(small, -1), ((1,), (1,)))
            second_acc[...] = part if j + i == 0 else second_acc[...] + part
    tall = own_a * 2 * PER
    row = lax.broadcasted_iota(jnp.int32, (tall, big), 0)
    col = lax.broadcasted_iota(jnp.int32, (tall, big), 1)
    keep = row % (2 * PER) == col % (2 * PER)
    source = lax.broadcasted_iota(jnp.int32, (big, 128), 0) // (2 * PER)
    source = ((source // own_a) ^ index[0]) * own_a + source % own_a
    lane = lax.broadcasted_iota(jnp.int32, (big, 128), 1)
    selector = (lane == source).astype(BF16)
    for block in range(n):
        picked = jnp.where(keep, third_acc[rows_of(index[0] ^ block, tall), :], 0.0)
        found = split_dot(picked, selector)
        total = found[: 2 * PER]
        for i in range(1, own_a):
            total += pltpu.roll(found[i * 2 * PER : (i + 1) * 2 * PER], i * A, 1)
        sums[block * PER : (block + 1) * PER, :] = total[:PER] + total[PER:]
    row = lax.broadcasted_iota(jnp.int32, (2 * PER, small), 0)
    col = lax.broadcasted_iota(jnp.int32, (2 * PER, small), 1)
    keep = row % PER == col % PER
    expand = lax.broadcasted_iota(jnp.int32, (small, 128), 0) // PER
    lane = lax.broadcasted_iota(jnp.int32, (small, 128), 1)
    total = 0.0
    for g in range(small // (2 * PER)):
        picked = jnp.where(keep, second_acc[g * 2 * PER : (g + 1) * 2 * PER, :], 0.0)
        total += split_dot(picked, (lane == expand + g * B).astype(BF16))
    sums[n * PER :, :] = total


def gate_grad_kernel(m, index, *refs):
    gathered, pre_grad, out = refs[:m], refs[m], refs[m + 1]
    width = pre_grad.shape[1]

    @pl.when(pl.program_id(0) == 0)
    def _():
        out[...] = jnp.zeros_like(out)

    for j in range(m):
        out[rows_of(index[1] ^ j, width), :] += dot(
            gathered[j][...], pre_grad[...], ((0,), (0,))
        )


def gate_input_kernel(m, index, *refs):
    grads, weights, upstream, out = refs[:m], refs[m : 2 * m], refs[2 * m], refs[2 * m + 1]
    total = upstream[...].astype(F32)
    for j in range(m):
        total += dot(grads[j][...], weights[j][...], ((1,), (1,)))
    out[...] = total


def first_grad_kernel(n, index, *refs):
    pieces, (tokens, back, out, held) = refs[:n], refs[n:]

    @pl.when(pl.program_id(0) == 0)
    def _():
        out[...] = jnp.zeros_like(out)

    for pair in range(B // 2):
        gather_rows(held.at[pair % 2], pieces, index[0], pair)
        sides = []
        for side in range(2):
            rows = slice((2 * pair + side) * C, (2 * pair + side + 1) * C)
            value = held[pair % 2, side].astype(BF16)
            back[rows, :] = value
            sides.append(dot(value, tokens[rows, :], ((1,), (1,))))
        both = jnp.concatenate(sides, 1).reshape(C // PER, PER, 2 * C)
        out[:, pair] += both


def input_grad_kernel(index, back, factor, partial, out):
    for b in range(B):
        rows = slice(b * C, (b + 1) * C)
        mixed = dot(factor[b], back[rows, :], ((0,), (0,)))
        out[rows, :] = (partial[rows, :] + mixed).astype(BF16)


def spread_diagonal(values, copies):
    rows, c, cols = values.shape
    tall = jnp.broadcast_to(values[:, None], (rows, copies, c, cols))
    tall = tall.reshape(rows * copies * c, cols)
    wide = cols * copies * c
    expand = (
        lax.broadcasted_iota(jnp.int32, (cols, wide), 1) // (copies * c)
        == lax.broadcasted_iota(jnp.int32, (cols, wide), 0)
    ).astype(BF16)
    dims = (tall.shape[0], wide)
    keep = (
        lax.broadcasted_iota(jnp.int32, dims, 0) % (copies * c)
        == lax.broadcasted_iota(jnp.int32, dims, 1) % (copies * c)
    )
    return jnp.where(keep, dot(tall, expand), 0.0).astype(BF16)


def resident(tokens, cotangent, first_factor, second_factor, third_factor, gate_weight):
    n = lax.axis_size("seq")
    s = lax.axis_index("seq")
    m = lax.axis_size("ch")
    q = lax.axis_index("ch")
    rows, width = tokens.shape
    own_a = rows // (B * C)
    index = jnp.stack([s, q]).astype(jnp.int32)
    piece = shape((own_a, B // 2, 2 * PER, width), BF16)
    piece_rows = [by_row(piece, own_a)] * n
    row_blocks = by_row(tokens, own_a)
    pair_rows = pltpu.VMEM((2, 2, C, width), F32)

    far_tokens = swap(tokens, "ch", 2)
    sent = call(
        first_kernel, (own_a,), index, (tokens, first_factor),
        [row_blocks, whole(first_factor)], [piece] * n, piece_rows, [pair_rows],
        2 * rows * width * C,
    )
    first_far = exchange(sent)
    gathered = [tokens, swap(tokens, "ch", 1), far_tokens, swap(far_tokens, "ch", 1)]
    weight_rows = [
        lax.dynamic_slice_in_dim(gate_weight, (q ^ j) * width, width, 0) for j in range(m)
    ]
    back_weight = [weight_rows[0]] + [swap(weight_rows[j], "ch", j) for j in range(1, m)]

    second_own = lax.dynamic_slice_in_dim(second_factor, s * PER, PER, 0)
    third_own = lax.dynamic_slice_in_dim(third_factor, s * PER, PER, 0)
    third_own = third_own.reshape(PER, n, own_a, n, own_a)
    third_own = flip_blocks(flip_blocks(third_own, 1, s), 3, s).reshape(PER, A, A)
    second_big = spread_diagonal(second_own.transpose(1, 0, 2), 1)
    third_big = spread_diagonal(third_own.transpose(1, 0, 2), 2)
    second_back = spread_diagonal(second_own.transpose(2, 0, 1), 1)
    third_back = spread_diagonal(third_own.transpose(2, 0, 1), 2)

    far = shape((A, B // 2, 2 * PER, width), BF16)
    ins = (*first_far, second_big, third_big)
    outs = [far] + [piece] * n
    second_far, *sent = call(
        functools.partial(far_kernel, n, own_a), (1,), index, ins,
        [whole(x) for x in ins], outs, [whole(x) for x in outs],
        (), 2 * rows * width * 6 * C,
    )
    mixed_home = exchange(sent)

    gate_shape = shape((rows, width), F32)
    ins = (*gathered, gate_weight, cotangent)
    gate_pre, *sent = call(
        functools.partial(gate_kernel, m), (own_a,), index, ins,
        [row_blocks] * m + [whole(gate_weight), row_blocks],
        [gate_shape] + [piece] * n, [row_blocks] + piece_rows, [pair_rows],
        2 * rows * width * m * width,
    )
    grad_far = exchange(sent)

    ins = (*mixed_home, gate_pre, tokens, cotangent)
    output, pre_grad = call(
        functools.partial(output_kernel, n), (own_a,), index, ins,
        piece_rows + [row_blocks] * 3, [shape((rows, width), BF16)] * 2, [row_blocks] * 2,
        [pair_rows], rows * width * 16,
    )
    far_pre = swap(pre_grad, "ch", 2)
    all_pre = [pre_grad, swap(pre_grad, "ch", 1), far_pre, swap(far_pre, "ch", 1)]

    ins = (*grad_far, second_back, third_back)
    outs = [far] + [piece] * n
    back_second, *sent = call(
        functools.partial(back_kernel, n, own_a), (1,), index, ins,
        [whole(x) for x in ins], outs, [whole(x) for x in outs], (),
        2 * rows * width * 6 * C,
    )
    back_home = exchange(sent)
    ins = (*grad_far, *first_far, second_far, back_second)
    outs = [shape((n * PER + 2 * PER, 128), F32)]
    sums = call(
        functools.partial(far_grad_kernel, n, own_a), (1,), index, ins,
        [whole(x) for x in ins], outs, [whole(x) for x in outs],
        [
            pltpu.VMEM((2 * A * PER, 2 * A * PER), F32),
            pltpu.VMEM((B * PER, B * PER), F32),
        ],
        2 * rows * width * 10 * C,
    )[0]

    out = shape((m * width, width), F32)
    gate_part = call(
        functools.partial(gate_grad_kernel, m), (own_a,), index, (*gathered, pre_grad),
        [row_blocks] * (m + 1), [out], [whole(out)], (),
        2 * rows * width * m * width,
    )[0].reshape(n, m * width // n, width)
    bit = 1
    while bit < n:
        mine = (s // bit) % 2
        split = gate_part.reshape(n // (2 * bit), 2, *gate_part.shape[1:])
        keep = lax.dynamic_index_in_dim(split, mine, 1, False)
        send = lax.dynamic_index_in_dim(split, 1 - mine, 1, False)
        gate_part = keep + swap(send, "seq", bit)
        bit *= 2
    gate_grad = gate_part.reshape(m * width // n, width)

    ins = (*all_pre, *back_weight, cotangent)
    partial = call(
        functools.partial(gate_input_kernel, m), (own_a,), index, ins,
        [row_blocks] * m + [whole(w) for w in back_weight] + [row_blocks],
        [gate_shape], [row_blocks], (), 2 * rows * width * m * width,
    )[0]

    bit = m // 2
    while bit:
        sums = sums + swap(sums, "ch", bit)
        bit //= 2
    every = sums.astype(BF16)[None]
    bit = 1
    while bit < n:
        other = swap(every, "seq", bit)
        every = jnp.where(
            (s // bit) % 2 == 1,
            jnp.concatenate([other, every], 0),
            jnp.concatenate([every, other], 0),
        )
        bit *= 2
    third_all = every[:, : n * PER].reshape(n, n, PER, 128).transpose(0, 2, 1, 3)
    third_grad = third_all.reshape(C, A, A)
    second_all = every[:, n * PER :].reshape(n, 2, PER, B // 2, B)
    second_grad = second_all.transpose(0, 2, 3, 1, 4).reshape(C, B, B)

    ins = (*back_home, tokens)
    first_out = shape((n, B // 2, PER, 2 * C), F32)
    back_rows, first_part = call(
        functools.partial(first_grad_kernel, n), (own_a,), index, ins,
        piece_rows + [row_blocks], [shape((rows, width), BF16), first_out],
        [row_blocks, whole(first_out)], [pair_rows], 2 * rows * width * C,
    )
    parts = first_part.reshape(n * m, -1, 128)
    parts = lax.all_to_all(parts, ("seq", "ch"), split_axis=0, concat_axis=0, tiled=True)
    first_sum = parts.sum(0).astype(BF16)
    first_sum = lax.all_to_all(
        jnp.broadcast_to(first_sum[None], (n * m, *first_sum.shape)),
        ("seq", "ch"), split_axis=0, concat_axis=0, tiled=True,
    )
    first_grad = first_sum.reshape(n, B // 2, PER, 2, C).transpose(1, 3, 0, 2, 4)
    first_grad = first_grad.reshape(B, C, C)

    ins = (back_rows, first_factor, partial)
    input_grad = call(
        input_grad_kernel, (own_a,), index, ins,
        [row_blocks, whole(first_factor), row_blocks],
        [shape((rows, width), BF16)], [row_blocks], (), 2 * rows * width * C,
    )[0]
    return output, input_grad, first_grad, second_grad, third_grad, gate_grad


def spread_out(tokens, cotangent, first_factor, second_factor, third_factor, gate_weight):
    seq_count = lax.axis_size("seq")
    seq_index = lax.axis_index("seq")
    per_device_c = max(1, C // seq_count)
    splits = max(1, seq_count // C)
    local_rows, width = tokens.shape
    narrow = width // splits
    blocks = local_rows // C
    batch_b = min(blocks, B)
    start_b = seq_index * blocks % B
    if blocks >= B:
        first_sel = first_factor
    else:
        first_sel = lax.dynamic_slice_in_dim(first_factor, start_b, blocks, 0)
    column = seq_index // splits * per_device_c
    second_sel = lax.dynamic_slice_in_dim(second_factor, column, per_device_c, 0)
    third_sel = lax.dynamic_slice_in_dim(third_factor, column, per_device_c, 0)
    grid_view = tokens.reshape(blocks // batch_b, batch_b, C, width)
    mixed_first = jnp.einsum(
        "bcd,ibdh->ibch", first_sel, grid_view, preferred_element_type=jnp.float32
    ).astype(jnp.bfloat16)

    def spread(values):
        return values.reshape(blocks, seq_count, per_device_c, narrow)

    received = lax.all_to_all(spread(mixed_first), "seq", split_axis=1, concat_axis=0, tiled=True)
    item_count = received.shape[3]
    far_view = received.reshape(A, B, per_device_c, item_count)
    second_val = jnp.einsum(
        "kbe,aekh->abkh", second_sel, far_view, preferred_element_type=jnp.float32
    ).astype(jnp.bfloat16)
    third_val = jnp.einsum(
        "kae,ebkh->abkh", third_sel, second_val, preferred_element_type=jnp.float32
    ).astype(jnp.bfloat16)
    first_far = received
    second_far = second_val.reshape(A * B, 1, per_device_c, item_count)
    mixed_far = third_val.reshape(A * B, 1, per_device_c, item_count)
    mixed_back = lax.all_to_all(mixed_far, "seq", split_axis=0, concat_axis=1, tiled=True).reshape(
        local_rows, width
    )
    full_tokens, full_weight = (
        lax.all_gather(tokens, "ch", axis=1, tiled=True),
        lax.all_gather(gate_weight, "ch", axis=1, tiled=True),
    )
    own_rows = lax.dynamic_slice_in_dim(full_weight, lax.axis_index("ch") * width, width, 0)
    gate_pre = jnp.dot(full_tokens, gate_weight, preferred_element_type=jnp.float32)
    sigmoid_gate = jax.nn.sigmoid(gate_pre)
    activation = gate_pre * sigmoid_gate
    mixed_float = mixed_back.astype(jnp.float32)
    output = (tokens.astype(jnp.float32) + mixed_float * activation).astype(jnp.bfloat16)
    upstream = cotangent.astype(jnp.float32)
    mix_grad = (upstream * activation).astype(jnp.bfloat16)
    pre_grad = (
        upstream * mixed_float * sigmoid_gate * (1.0 + gate_pre * (1.0 - sigmoid_gate))
    ).astype(jnp.bfloat16)
    received = lax.all_to_all(spread(mix_grad), "seq", split_axis=1, concat_axis=0, tiled=True)
    item_count = received.shape[3]
    far_view = received.reshape(A, B, per_device_c, item_count)
    back_second = jnp.einsum(
        "kae,abkh->ebkh", third_sel, far_view, preferred_element_type=jnp.float32
    ).astype(jnp.bfloat16)
    back_first = jnp.einsum(
        "kbe,abkh->aekh", second_sel, back_second, preferred_element_type=jnp.float32
    ).astype(jnp.bfloat16)
    second_back = back_second.reshape(A * B, 1, per_device_c, item_count)
    first_back = back_first.reshape(A * B, 1, per_device_c, item_count)
    third_part = jnp.einsum(
        "abkh,ebkh->kae",
        received.reshape(A, B, per_device_c, narrow),
        second_far.reshape(A, B, per_device_c, narrow),
        preferred_element_type=jnp.float32,
    )
    second_part = jnp.einsum(
        "abkh,aekh->kbe",
        second_back.reshape(A, B, per_device_c, narrow),
        first_far.reshape(A, B, per_device_c, narrow),
        preferred_element_type=jnp.float32,
    )
    first_home = lax.all_to_all(first_back, "seq", split_axis=0, concat_axis=1, tiled=True).reshape(
        blocks // batch_b, batch_b, C, width
    )
    mix_input = jnp.einsum(
        "bcd,ibch->ibdh", first_sel, first_home, preferred_element_type=jnp.float32
    ).reshape(local_rows, width)
    first_part = jnp.einsum(
        "ibch,ibdh->bcd", first_home, grid_view, preferred_element_type=jnp.float32
    )
    if blocks >= B:
        first_full = first_part
    else:
        first_full = lax.dynamic_update_slice_in_dim(
            jnp.zeros((B, C, C), jnp.float32), first_part, start_b, 0
        )
    second_full = lax.dynamic_update_slice_in_dim(
        jnp.zeros((C, B, B), jnp.float32), second_part, column, 0
    )
    third_full = lax.dynamic_update_slice_in_dim(
        jnp.zeros((C, A, A), jnp.float32), third_part, column, 0
    )
    first_sum, second_sum, third_sum = lax.psum(
        (first_full, second_full, third_full), ("seq", "ch")
    )
    gate_input = lax.dot_general(
        lax.all_gather(pre_grad, "ch", axis=1, tiled=True),
        own_rows,
        (((1,), (1,)), ((), ())),
        preferred_element_type=jnp.float32,
    )
    gate_grad = lax.psum_scatter(
        lax.dot_general(
            full_tokens, pre_grad, (((0,), (0,)), ((), ())), preferred_element_type=jnp.float32
        ),
        "seq",
        scatter_dimension=0,
        tiled=True,
    )
    input_grad = (upstream + mix_input + gate_input).astype(jnp.bfloat16)
    return (
        output,
        input_grad,
        first_sum.astype(jnp.bfloat16),
        second_sum.astype(jnp.bfloat16),
        third_sum.astype(jnp.bfloat16),
        gate_grad,
    )


def on_device(*arrays):
    n = lax.axis_size("seq")
    rows = arrays[0].shape[0]
    square = lax.axis_size("ch") == 4 and n * PER == C
    if square and rows % (B * C) == 0 and rows * n == A * B * C:
        return resident(*arrays)
    return spread_out(*arrays)


def solution(mesh):
    placed = (P("seq", "ch"), P("seq", "ch"), P(), P(), P(), P(None, "ch"))
    return jax.shard_map(
        on_device,
        mesh=mesh,
        in_specs=placed,
        out_specs=(P("seq", "ch"), P("seq", "ch"), P(), P(), P(), P("seq", "ch")),
        check_vma=False,
    )
```

```python
import functools

import jax
import jax.numpy as jnp
from jax import lax
from jax.experimental import pallas as pl
from jax.experimental.pallas import tpu as pltpu
from jax.sharding import PartitionSpec as P

A = 32
B = 16
C = 64
PER = 8
F32 = jnp.float32
BF16 = jnp.bfloat16
HALVES = 2
BACK_HALVES = 1
VMEM_BYTES = 56 * 1024 * 1024


def swap(values, axis, step):
    count = lax.axis_size(axis)
    return lax.ppermute(values, axis, [(i, i ^ step) for i in range(count)])


def exchange(pieces):
    moved = {}
    for j in range(len(pieces) - 1, 0, -1):
        moved[j] = swap(pieces[j], "seq", j)
    return [pieces[0]] + [moved[j] for j in range(1, len(pieces))]


def dot(left, right, dims=((1,), (0,))):
    return lax.dot_general(left, right, (dims, ((), ())), preferred_element_type=F32)


def rows_of(block, count):
    return pl.ds(pl.multiple_of(block * count, count), count)


def call(kernel, grid, index, ins, in_specs, outs, out_specs, scratch=(), flops=0):
    moved = sum(x.size * x.dtype.itemsize for x in list(ins) + list(outs))
    return pl.pallas_call(
        kernel,
        grid_spec=pltpu.PrefetchScalarGridSpec(
            num_scalar_prefetch=1,
            grid=grid,
            in_specs=in_specs,
            out_specs=out_specs,
            scratch_shapes=scratch,
        ),
        out_shape=outs,
        compiler_params=pltpu.CompilerParams(
            dimension_semantics=("arbitrary",) * len(grid), vmem_limit_bytes=VMEM_BYTES
        ),
        cost_estimate=pl.CostEstimate(flops=flops, transcendentals=0, bytes_accessed=moved),
    )(index, *ins)


def shape(dims, dtype):
    return jax.ShapeDtypeStruct(dims, dtype)


def whole(x):
    dims = x.shape
    return pl.BlockSpec(dims, lambda *_: (0,) * len(dims))


def by_row(x, parts):
    dims = (x.shape[0] // parts,) + tuple(x.shape[1:])
    return pl.BlockSpec(dims, lambda i, *_: (i,) + (0,) * (len(dims) - 1))


def scatter_rows(source, pieces, me, pair, columns=slice(None)):
    for j, piece in enumerate(pieces):
        low = source[0, rows_of(me ^ j, PER), columns]
        high = source[1, rows_of(me ^ j, PER), columns]
        piece[0, pair] = jnp.concatenate([low, high], 0).astype(BF16)


def gather_rows(target, pieces, me, pair, columns=slice(None)):
    for j, piece in enumerate(pieces):
        both = piece[0, pair].astype(F32)
        target[0, rows_of(me ^ j, PER), columns] = both[:PER]
        target[1, rows_of(me ^ j, PER), columns] = both[PER:]


def first_kernel(index, tokens, factor, *rest):
    pieces, held = rest[:-1], rest[-1]
    for pair in range(B // 2):
        for side in range(2):
            b = 2 * pair + side
            held[pair % 2, side] = dot(factor[b], tokens[b * C : (b + 1) * C, :])
        scatter_rows(held.at[pair % 2], pieces, index[0], pair)


def far_kernel(n, own_a, index, *refs):
    first, (second_big, third_big), second_out, pieces = (
        refs[:n], refs[n : n + 2], refs[n + 2], refs[n + 3 :]
    )
    for j in range(n):
        for i in range(own_a):
            block = first[j][i].reshape(B * PER, -1)
            mixed = dot(second_big[...], block).astype(BF16)
            second_out[j * own_a + i] = mixed.reshape(second_out.shape[1:])
    for pair in range(B // 2):
        block = second_out[:, pair].reshape(2 * A * PER, -1)
        mixed = dot(third_big[...], block).astype(BF16).reshape(A, 2 * PER, -1)
        for j in range(n):
            pieces[j][:, pair] = mixed[j * own_a : (j + 1) * own_a]


def gate_kernel(m, index, *refs):
    gathered, (weight, upstream, gate_out), pieces, held = (
        refs[:m], refs[m : m + 3], refs[m + 3 : -1], refs[-1]
    )
    width = weight.shape[1]
    for pair in range(B // 2):
        rows = slice(pair * 2 * C, (pair + 1) * 2 * C)
        gate = 0.0
        for j in range(m):
            gate += dot(gathered[j][rows, :], weight[rows_of(index[1] ^ j, width), :])
        gate_out[rows, :] = gate
        grad = upstream[rows, :].astype(F32) * (gate * jax.nn.sigmoid(gate))
        held[pair % 2] = grad.reshape(2, C, width)
        count = len(pieces) // BACK_HALVES
        for h in range(BACK_HALVES):
            columns = slice(h * width // BACK_HALVES, (h + 1) * width // BACK_HALVES)
            some = pieces[h * count : (h + 1) * count]
            scatter_rows(held.at[pair % 2], some, index[0], pair, columns)


def output_kernel(n, index, *refs):
    pieces, (gate_in, tokens, upstream, output, pre_grad, held) = refs[:-6], refs[-6:]
    for pair in range(B // 2):
        rows = slice(pair * 2 * C, (pair + 1) * 2 * C)
        for h in range(len(pieces) // n):
            some = pieces[h * n : (h + 1) * n]
            step = some[0].shape[-1]
            columns = slice(h * step, (h + 1) * step)
            gather_rows(held.at[pair % 2], some, index[0], pair, columns)
        mixed = held[pair % 2].reshape(2 * C, -1)
        gate = gate_in[rows, :]
        sig = jax.nn.sigmoid(gate)
        output[rows, :] = (tokens[rows, :].astype(F32) + mixed * (gate * sig)).astype(BF16)
        pre_grad[rows, :] = (
            upstream[rows, :].astype(F32) * mixed * sig * (1.0 + gate * (1.0 - sig))
        ).astype(BF16)


def split_dot(values, selector):
    top = values.astype(BF16)
    rest = values - top.astype(F32)
    middle = rest.astype(BF16)
    low = (rest - middle.astype(F32)).astype(BF16)
    return dot(top, selector) + dot(middle, selector) + dot(low, selector)


def back_kernel(n, own_a, index, *refs):
    grads, (second_big, third_big, back_second), pieces = refs[:n], refs[n : n + 3], refs[n + 3 :]
    for pair in range(B // 2):
        block = jnp.concatenate([g[:, pair].reshape(own_a * 2 * PER, -1) for g in grads], 0)
        back = dot(third_big[...], block).astype(BF16)
        back_second[:, pair] = back.reshape(A, 2 * PER, -1)
    for j in range(n):
        for i in range(own_a):
            block = back_second[j * own_a + i].reshape(B * PER, -1)
            pieces[j][i] = dot(second_big[...], block).astype(BF16).reshape(pieces[j].shape[1:])


def far_grad_kernel(n, own_a, index, *refs):
    cuts = [BACK_HALVES * n, HALVES * n, HALVES, BACK_HALVES]
    ends = [sum(cuts[: k + 1]) for k in range(4)]
    grads, first = refs[: ends[0]], refs[ends[0] : ends[1]]
    second_vals, back_vals = refs[ends[1] : ends[2]], refs[ends[2] : ends[3]]
    sums, third_acc, second_acc = refs[ends[3] :]
    big = 2 * A * PER
    small = B * PER

    def wide(blocks):
        return blocks[0] if len(blocks) == 1 else jnp.concatenate(blocks, 1)

    for pair in range(B // 2):
        sides = []
        for h in range(BACK_HALVES):
            some = grads[h * n : (h + 1) * n]
            sides.append(
                jnp.concatenate([g[:, pair].reshape(own_a * 2 * PER, -1) for g in some], 0)
            )
        other = wide([v[:, pair].reshape(big, -1) for v in second_vals])
        part = dot(wide(sides), other, ((1,), (1,)))
        third_acc[...] = part if pair == 0 else third_acc[...] + part
    for j in range(n):
        for i in range(own_a):
            block = wide([v[j * own_a + i].reshape(small, -1) for v in back_vals])
            other = wide([first[h * n + j][i].reshape(small, -1) for h in range(HALVES)])
            part = dot(block, other, ((1,), (1,)))
            second_acc[...] = part if j + i == 0 else second_acc[...] + part
    tall = own_a * 2 * PER
    row = lax.broadcasted_iota(jnp.int32, (tall, big), 0)
    col = lax.broadcasted_iota(jnp.int32, (tall, big), 1)
    keep = row % (2 * PER) == col % (2 * PER)
    source = lax.broadcasted_iota(jnp.int32, (big, 128), 0) // (2 * PER)
    source = ((source // own_a) ^ index[0]) * own_a + source % own_a
    lane = lax.broadcasted_iota(jnp.int32, (big, 128), 1)
    selector = (lane == source).astype(BF16)
    for block in range(n):
        picked = jnp.where(keep, third_acc[rows_of(index[0] ^ block, tall), :], 0.0)
        found = split_dot(picked, selector)
        total = found[: 2 * PER]
        for i in range(1, own_a):
            total += pltpu.roll(found[i * 2 * PER : (i + 1) * 2 * PER], i * A, 1)
        sums[block * PER : (block + 1) * PER, :] = total[:PER] + total[PER:]
    row = lax.broadcasted_iota(jnp.int32, (2 * PER, small), 0)
    col = lax.broadcasted_iota(jnp.int32, (2 * PER, small), 1)
    keep = row % PER == col % PER
    expand = lax.broadcasted_iota(jnp.int32, (small, 128), 0) // PER
    lane = lax.broadcasted_iota(jnp.int32, (small, 128), 1)
    total = 0.0
    for g in range(small // (2 * PER)):
        picked = jnp.where(keep, second_acc[g * 2 * PER : (g + 1) * 2 * PER, :], 0.0)
        total += split_dot(picked, (lane == expand + g * B).astype(BF16))
    sums[n * PER :, :] = total


def gate_grad_kernel(m, index, *refs):
    gathered, pre_grad, out = refs[:m], refs[m], refs[m + 1]
    width = pre_grad.shape[1]

    @pl.when(pl.program_id(0) == 0)
    def _():
        out[...] = jnp.zeros_like(out)

    for j in range(m):
        out[rows_of(index[1] ^ j, width), :] += dot(
            gathered[j][...], pre_grad[...], ((0,), (0,))
        )


def gate_input_kernel(m, index, *refs):
    grads, weights, upstream, out = refs[:m], refs[m : 2 * m], refs[2 * m], refs[2 * m + 1]
    total = upstream[...].astype(F32)
    for j in range(m):
        total += dot(grads[j][...], weights[j][...], ((1,), (1,)))
    out[...] = total


def first_grad_kernel(n, index, *refs):
    pieces, (tokens, back, out, held, total) = refs[:n], refs[n:]

    @pl.when(pl.program_id(0) == 0)
    def _():
        total[...] = jnp.zeros_like(total)

    for pair in range(B // 2):
        gather_rows(held.at[pair % 2], pieces, index[0], pair)
        sides = []
        for side in range(2):
            rows = slice((2 * pair + side) * C, (2 * pair + side + 1) * C)
            value = held[pair % 2, side].astype(BF16)
            back[rows, :] = value
            sides.append(dot(value, tokens[rows, :], ((1,), (1,))))
        both = jnp.concatenate(sides, 1).reshape(C // PER, PER, 2 * C)
        total[:, pair] += both

    @pl.when(pl.program_id(0) == pl.num_programs(0) - 1)
    def _():
        out[...] = total[...].reshape(out.shape).astype(out.dtype)


def input_grad_kernel(index, *refs):
    back, (factor, partial, out) = refs[:-3], refs[-3:]
    for b in range(B):
        rows = slice(b * C, (b + 1) * C)
        value = [x[rows, :] for x in back]
        value = value[0] if len(value) == 1 else jnp.concatenate(value, 1)
        mixed = dot(factor[b], value, ((0,), (0,)))
        out[rows, :] = (partial[rows, :] + mixed).astype(BF16)


def one_hot(dims, test):
    return test(
        lax.broadcasted_iota(jnp.int32, dims, 0), lax.broadcasted_iota(jnp.int32, dims, 1)
    ).astype(BF16)


def spread_kernel(own_a, back, index, third, second, third_big, second_big):
    me = index[0]

    def place(slot):
        return ((slot // own_a) ^ me) * own_a + slot % own_a

    def fill(values, copies, count, big, where):
        fast = copies * PER
        size = count * fast
        rows = one_hot(
            (size, PER * count), lambda r, k: k == (r % PER) * count + where(r // fast)
        )
        columns = one_hot((size, count), lambda r, k: k == where(r // fast))
        if back:
            picked = dot(columns, values, ((1,), (1,))).astype(BF16)
            wide = dot(picked, rows, ((1,), (1,)))
        else:
            picked = dot(rows, values).astype(BF16)
            wide = dot(picked, columns, ((1,), (1,)))
        row = lax.broadcasted_iota(jnp.int32, (size, size), 0)
        col = lax.broadcasted_iota(jnp.int32, (size, size), 1)
        big[...] = jnp.where(row % fast == col % fast, wide, 0.0).astype(BF16)

    own = third[pl.ds(pl.multiple_of(me * PER, PER), PER)].reshape(PER * A, A)
    fill(own, 2, A, third_big, place)
    own = second[pl.ds(pl.multiple_of(me * PER, PER), PER)].reshape(PER * B, B)
    fill(own, 1, B, second_big, lambda slot: slot)


def resident(tokens, cotangent, first_factor, second_factor, third_factor, gate_weight):
    n = lax.axis_size("seq")
    s = lax.axis_index("seq")
    m = lax.axis_size("ch")
    q = lax.axis_index("ch")
    rows, width = tokens.shape
    own_a = rows // (B * C)
    index = jnp.stack([s, q]).astype(jnp.int32)
    row_blocks = by_row(tokens, own_a)
    pair_rows = pltpu.VMEM((2, 2, C, width), F32)

    far_tokens = swap(tokens, "ch", 2)
    half_width = width // HALVES
    half = shape((own_a, B // 2, 2 * PER, half_width), BF16)
    half_rows = [by_row(half, own_a)] * n
    part_width = width // BACK_HALVES
    part = shape((own_a, B // 2, 2 * PER, part_width), BF16)
    part_rows = [by_row(part, own_a)] * n
    far_part = shape((A, B // 2, 2 * PER, part_width), BF16)
    first_far = []
    for h in range(HALVES):
        columns = pl.BlockSpec((B * C, half_width), lambda i, *_, h=h: (i, h))
        sent = call(
            first_kernel, (own_a,), index, (tokens, first_factor),
            [columns, whole(first_factor)], [half] * n, half_rows,
            [pltpu.VMEM((2, 2, C, half_width), F32)],
            2 * rows * half_width * C,
        )
        first_far.append(exchange(sent))
    gathered = [tokens, swap(tokens, "ch", 1), far_tokens, swap(far_tokens, "ch", 1)]
    weight_rows = [
        lax.dynamic_slice_in_dim(gate_weight, (q ^ j) * width, width, 0) for j in range(m)
    ]
    back_weight = [weight_rows[0]] + [swap(weight_rows[j], "ch", j) for j in range(1, m)]

    spread = []
    for back in (False, True):
        ins = (third_factor, second_factor)
        outs = [shape((2 * A * PER,) * 2, BF16), shape((B * PER,) * 2, BF16)]
        spread += call(
            functools.partial(spread_kernel, own_a, back), (1,), index, ins,
            [whole(x) for x in ins], outs, [whole(x) for x in outs], (),
            0,
        )
    third_big, second_big, third_back, second_back = spread

    far_half = shape((A, B // 2, 2 * PER, half_width), BF16)
    second_far, mixed_home = [], []
    for h in range(HALVES):
        ins = (*first_far[h], second_big, third_big)
        outs = [far_half] + [half] * n
        second_val, *sent = call(
            functools.partial(far_kernel, n, own_a), (1,), index, ins,
            [whole(x) for x in ins], outs, [whole(x) for x in outs],
            (), 2 * rows * half_width * 6 * C,
        )
        second_far.append(second_val)
        mixed_home += exchange(sent)

    gate_shape = shape((rows, width), F32)
    ins = (*gathered, gate_weight, cotangent)
    gate_pre, *sent = call(
        functools.partial(gate_kernel, m), (own_a,), index, ins,
        [row_blocks] * m + [whole(gate_weight), row_blocks],
        [gate_shape] + [part] * (n * BACK_HALVES),
        [row_blocks] + part_rows * BACK_HALVES, [pair_rows],
        2 * rows * width * m * width,
    )
    grad_far = [exchange(sent[h * n : (h + 1) * n]) for h in range(BACK_HALVES)]

    ins = (*mixed_home, gate_pre, tokens, cotangent)
    output, pre_grad = call(
        functools.partial(output_kernel, n), (own_a,), index, ins,
        half_rows * HALVES + [row_blocks] * 3,
        [shape((rows, width), BF16)] * 2, [row_blocks] * 2,
        [pair_rows], rows * width * 16,
    )
    far_pre = swap(pre_grad, "ch", 2)
    all_pre = [pre_grad, swap(pre_grad, "ch", 1), far_pre, swap(far_pre, "ch", 1)]

    back_home, back_far = [], []
    for h in range(BACK_HALVES):
        ins = (*grad_far[h], second_back, third_back)
        outs = [far_part] + [part] * n
        back_second, *sent = call(
            functools.partial(back_kernel, n, own_a), (1,), index, ins,
            [whole(x) for x in ins], outs, [whole(x) for x in outs], (),
            2 * rows * part_width * 6 * C,
        )
        back_far.append(back_second)
        back_home.append(exchange(sent))

    def flat(halves):
        return [x for half_pieces in halves for x in half_pieces]

    ins = (*flat(grad_far), *flat(first_far), *second_far, *back_far)
    outs = [shape((n * PER + 2 * PER, 128), F32)]
    sums = call(
        functools.partial(far_grad_kernel, n, own_a), (1,), index, ins,
        [whole(x) for x in ins], outs, [whole(x) for x in outs],
        [
            pltpu.VMEM((2 * A * PER, 2 * A * PER), F32),
            pltpu.VMEM((B * PER, B * PER), F32),
        ],
        2 * rows * width * 10 * C,
    )[0]

    out = shape((m * width, width), F32)
    gate_part = call(
        functools.partial(gate_grad_kernel, m), (own_a,), index, (*gathered, pre_grad),
        [row_blocks] * (m + 1), [out], [whole(out)], (),
        2 * rows * width * m * width,
    )[0].reshape(n, m * width // n, width)
    bit = 1
    while bit < n:
        mine = (s // bit) % 2
        split = gate_part.reshape(n // (2 * bit), 2, *gate_part.shape[1:])
        keep = lax.dynamic_index_in_dim(split, mine, 1, False)
        send = lax.dynamic_index_in_dim(split, 1 - mine, 1, False)
        gate_part = keep + swap(send, "seq", bit)
        bit *= 2
    gate_grad = gate_part.reshape(m * width // n, width)

    ins = (*all_pre, *back_weight, cotangent)
    partial = call(
        functools.partial(gate_input_kernel, m), (own_a,), index, ins,
        [row_blocks] * m + [whole(w) for w in back_weight] + [row_blocks],
        [gate_shape], [row_blocks], (), 2 * rows * width * m * width,
    )[0]

    bit = m // 2
    while bit:
        sums = sums + swap(sums, "ch", bit)
        bit //= 2
    every = jnp.broadcast_to(sums.astype(BF16)[None], (n, *sums.shape))
    every = lax.all_to_all(every, "seq", split_axis=0, concat_axis=0, tiled=True)
    third_all = every[:, : n * PER].reshape(n, n, PER, 128).transpose(0, 2, 1, 3)
    third_grad = third_all.reshape(C, A, A)
    second_all = every[:, n * PER :].reshape(n, 2, PER, B // 2, B)
    second_grad = second_all.transpose(0, 2, 3, 1, 4).reshape(C, B, B)

    first_out = shape((n * m, B * C // (2 * n * m), 2 * C), BF16)
    ins = (*back_home[0], tokens)
    back_rows, parts = call(
        functools.partial(first_grad_kernel, n), (own_a,), index, ins,
        part_rows + [row_blocks], [shape((rows, width), BF16), first_out],
        [row_blocks, whole(first_out)],
        [pair_rows, pltpu.VMEM((n, B // 2, PER, 2 * C), F32)],
        2 * rows * width * C,
    )
    parts = lax.all_to_all(parts, ("seq", "ch"), split_axis=0, concat_axis=0, tiled=True)
    first_sum = parts.astype(F32).sum(0).astype(BF16)
    first_sum = lax.all_to_all(
        jnp.broadcast_to(first_sum[None], (n * m, *first_sum.shape)),
        ("seq", "ch"), split_axis=0, concat_axis=0, tiled=True,
    )
    first_grad = first_sum.reshape(n, B // 2, PER, 2, C).transpose(1, 3, 0, 2, 4)
    first_grad = first_grad.reshape(B, C, C)

    ins = (back_rows, first_factor, partial)
    input_grad = call(
        input_grad_kernel, (own_a,), index, ins,
        [row_blocks, whole(first_factor), row_blocks],
        [shape((rows, width), BF16)], [row_blocks], (), 2 * rows * width * C,
    )[0]
    return output, input_grad, first_grad, second_grad, third_grad, gate_grad


def spread_out(tokens, cotangent, first_factor, second_factor, third_factor, gate_weight):
    seq_count = lax.axis_size("seq")
    seq_index = lax.axis_index("seq")
    per_device_c = max(1, C // seq_count)
    splits = max(1, seq_count // C)
    local_rows, width = tokens.shape
    narrow = width // splits
    blocks = local_rows // C
    batch_b = min(blocks, B)
    start_b = seq_index * blocks % B
    if blocks >= B:
        first_sel = first_factor
    else:
        first_sel = lax.dynamic_slice_in_dim(first_factor, start_b, blocks, 0)
    column = seq_index // splits * per_device_c
    second_sel = lax.dynamic_slice_in_dim(second_factor, column, per_device_c, 0)
    third_sel = lax.dynamic_slice_in_dim(third_factor, column, per_device_c, 0)
    grid_view = tokens.reshape(blocks // batch_b, batch_b, C, width)
    mixed_first = jnp.einsum(
        "bcd,ibdh->ibch", first_sel, grid_view, preferred_element_type=jnp.float32
    ).astype(jnp.bfloat16)

    def spread(values):
        return values.reshape(blocks, seq_count, per_device_c, narrow)

    received = lax.all_to_all(spread(mixed_first), "seq", split_axis=1, concat_axis=0, tiled=True)
    item_count = received.shape[3]
    far_view = received.reshape(A, B, per_device_c, item_count)
    second_val = jnp.einsum(
        "kbe,aekh->abkh", second_sel, far_view, preferred_element_type=jnp.float32
    ).astype(jnp.bfloat16)
    third_val = jnp.einsum(
        "kae,ebkh->abkh", third_sel, second_val, preferred_element_type=jnp.float32
    ).astype(jnp.bfloat16)
    first_far = received
    second_far = second_val.reshape(A * B, 1, per_device_c, item_count)
    mixed_far = third_val.reshape(A * B, 1, per_device_c, item_count)
    mixed_back = lax.all_to_all(mixed_far, "seq", split_axis=0, concat_axis=1, tiled=True).reshape(
        local_rows, width
    )
    full_tokens, full_weight = (
        lax.all_gather(tokens, "ch", axis=1, tiled=True),
        lax.all_gather(gate_weight, "ch", axis=1, tiled=True),
    )
    own_rows = lax.dynamic_slice_in_dim(full_weight, lax.axis_index("ch") * width, width, 0)
    gate_pre = jnp.dot(full_tokens, gate_weight, preferred_element_type=jnp.float32)
    sigmoid_gate = jax.nn.sigmoid(gate_pre)
    activation = gate_pre * sigmoid_gate
    mixed_float = mixed_back.astype(jnp.float32)
    output = (tokens.astype(jnp.float32) + mixed_float * activation).astype(jnp.bfloat16)
    upstream = cotangent.astype(jnp.float32)
    mix_grad = (upstream * activation).astype(jnp.bfloat16)
    pre_grad = (
        upstream * mixed_float * sigmoid_gate * (1.0 + gate_pre * (1.0 - sigmoid_gate))
    ).astype(jnp.bfloat16)
    received = lax.all_to_all(spread(mix_grad), "seq", split_axis=1, concat_axis=0, tiled=True)
    item_count = received.shape[3]
    far_view = received.reshape(A, B, per_device_c, item_count)
    back_second = jnp.einsum(
        "kae,abkh->ebkh", third_sel, far_view, preferred_element_type=jnp.float32
    ).astype(jnp.bfloat16)
    back_first = jnp.einsum(
        "kbe,abkh->aekh", second_sel, back_second, preferred_element_type=jnp.float32
    ).astype(jnp.bfloat16)
    second_back = back_second.reshape(A * B, 1, per_device_c, item_count)
    first_back = back_first.reshape(A * B, 1, per_device_c, item_count)
    third_part = jnp.einsum(
        "abkh,ebkh->kae",
        received.reshape(A, B, per_device_c, narrow),
        second_far.reshape(A, B, per_device_c, narrow),
        preferred_element_type=jnp.float32,
    )
    second_part = jnp.einsum(
        "abkh,aekh->kbe",
        second_back.reshape(A, B, per_device_c, narrow),
        first_far.reshape(A, B, per_device_c, narrow),
        preferred_element_type=jnp.float32,
    )
    first_home = lax.all_to_all(first_back, "seq", split_axis=0, concat_axis=1, tiled=True).reshape(
        blocks // batch_b, batch_b, C, width
    )
    mix_input = jnp.einsum(
        "bcd,ibch->ibdh", first_sel, first_home, preferred_element_type=jnp.float32
    ).reshape(local_rows, width)
    first_part = jnp.einsum(
        "ibch,ibdh->bcd", first_home, grid_view, preferred_element_type=jnp.float32
    )
    if blocks >= B:
        first_full = first_part
    else:
        first_full = lax.dynamic_update_slice_in_dim(
            jnp.zeros((B, C, C), jnp.float32), first_part, start_b, 0
        )
    second_full = lax.dynamic_update_slice_in_dim(
        jnp.zeros((C, B, B), jnp.float32), second_part, column, 0
    )
    third_full = lax.dynamic_update_slice_in_dim(
        jnp.zeros((C, A, A), jnp.float32), third_part, column, 0
    )
    first_sum, second_sum, third_sum = lax.psum(
        (first_full, second_full, third_full), ("seq", "ch")
    )
    gate_input = lax.dot_general(
        lax.all_gather(pre_grad, "ch", axis=1, tiled=True),
        own_rows,
        (((1,), (1,)), ((), ())),
        preferred_element_type=jnp.float32,
    )
    gate_grad = lax.psum_scatter(
        lax.dot_general(
            full_tokens, pre_grad, (((0,), (0,)), ((), ())), preferred_element_type=jnp.float32
        ),
        "seq",
        scatter_dimension=0,
        tiled=True,
    )
    input_grad = (upstream + mix_input + gate_input).astype(jnp.bfloat16)
    return (
        output,
        input_grad,
        first_sum.astype(jnp.bfloat16),
        second_sum.astype(jnp.bfloat16),
        third_sum.astype(jnp.bfloat16),
        gate_grad,
    )


def on_device(*arrays):
    n = lax.axis_size("seq")
    rows = arrays[0].shape[0]
    square = lax.axis_size("ch") == 4 and n * PER == C
    if square and rows % (B * C) == 0 and rows * n == A * B * C:
        return resident(*arrays)
    return spread_out(*arrays)


def solution(mesh):
    placed = (P("seq", "ch"), P("seq", "ch"), P(), P(), P(), P(None, "ch"))
    return jax.shard_map(
        on_device,
        mesh=mesh,
        in_specs=placed,
        out_specs=(P("seq", "ch"), P("seq", "ch"), P(), P(), P(), P("seq", "ch")),
        check_vma=False,
    )
```

```python
import functools

import jax
import jax.numpy as jnp
from jax import lax
from jax.experimental import pallas as pl
from jax.experimental.pallas import tpu as pltpu
from jax.sharding import PartitionSpec as P

A = 32
B = 16
C = 64
PER = 8
F32 = jnp.float32
BF16 = jnp.bfloat16
HALVES = 2
BACK_HALVES = 1
STEPS = 2
VMEM_BYTES = 56 * 1024 * 1024


def swap(values, axis, step):
    count = lax.axis_size(axis)
    return lax.ppermute(values, axis, [(i, i ^ step) for i in range(count)])


def exchange(pieces):
    moved = {}
    for j in range(len(pieces) - 1, 0, -1):
        moved[j] = swap(pieces[j], "seq", j)
    return [pieces[0]] + [moved[j] for j in range(1, len(pieces))]


def dot(left, right, dims=((1,), (0,))):
    return lax.dot_general(left, right, (dims, ((), ())), preferred_element_type=F32)


def rows_of(block, count):
    return pl.ds(pl.multiple_of(block * count, count), count)


def call(kernel, grid, index, ins, in_specs, outs, out_specs, scratch=(), flops=0):
    moved = sum(x.size * x.dtype.itemsize for x in list(ins) + list(outs))
    return pl.pallas_call(
        kernel,
        grid_spec=pltpu.PrefetchScalarGridSpec(
            num_scalar_prefetch=1,
            grid=grid,
            in_specs=in_specs,
            out_specs=out_specs,
            scratch_shapes=scratch,
        ),
        out_shape=outs,
        compiler_params=pltpu.CompilerParams(
            dimension_semantics=("arbitrary",) * len(grid), vmem_limit_bytes=VMEM_BYTES
        ),
        cost_estimate=pl.CostEstimate(flops=flops, transcendentals=0, bytes_accessed=moved),
    )(index, *ins)


def shape(dims, dtype):
    return jax.ShapeDtypeStruct(dims, dtype)


def whole(x):
    dims = x.shape
    return pl.BlockSpec(dims, lambda *_: (0,) * len(dims))


def by_row(x, parts):
    dims = (x.shape[0] // parts,) + tuple(x.shape[1:])
    return pl.BlockSpec(dims, lambda i, *_: (i,) + (0,) * (len(dims) - 1))


def blocks_of(ref):
    for i in range(ref.shape[0] // (B * C)):
        for pair in range(B // 2):
            yield (i * B + 2 * pair) * C, i, pair


def scatter_rows(source, pieces, me, i, pair, columns=slice(None)):
    for j, piece in enumerate(pieces):
        low = source[0, rows_of(me ^ j, PER), columns]
        high = source[1, rows_of(me ^ j, PER), columns]
        piece[i, pair] = jnp.concatenate([low, high], 0).astype(BF16)


def gather_rows(target, pieces, me, i, pair, columns=slice(None)):
    for j, piece in enumerate(pieces):
        both = piece[i, pair].astype(F32)
        target[0, rows_of(me ^ j, PER), columns] = both[:PER]
        target[1, rows_of(me ^ j, PER), columns] = both[PER:]


def first_kernel(index, tokens, factor, *rest):
    pieces, held = rest[:-1], rest[-1]
    for row, i, pair in blocks_of(tokens):
        for side in range(2):
            rows = slice(row + side * C, row + (side + 1) * C)
            held[pair % 2, side] = dot(factor[2 * pair + side], tokens[rows, :])
        scatter_rows(held.at[pair % 2], pieces, index[0], i, pair)


def far_kernel(n, own_a, index, *refs):
    first, (second_big, third_big), second_out, pieces = (
        refs[:n], refs[n : n + 2], refs[n + 2], refs[n + 3 :]
    )
    for j in range(n):
        for i in range(own_a):
            block = first[j][i].reshape(B * PER, -1)
            mixed = dot(second_big[...], block).astype(BF16)
            second_out[j * own_a + i] = mixed.reshape(second_out.shape[1:])
    for pair in range(B // 2):
        block = second_out[:, pair].reshape(2 * A * PER, -1)
        mixed = dot(third_big[...], block).astype(BF16).reshape(A, 2 * PER, -1)
        for j in range(n):
            pieces[j][:, pair] = mixed[j * own_a : (j + 1) * own_a]


def gate_kernel(m, index, *refs):
    gathered, (weight, upstream, gate_out), pieces, held = (
        refs[:m], refs[m : m + 3], refs[m + 3 : -1], refs[-1]
    )
    width = weight.shape[1]
    for row, i, pair in blocks_of(gate_out):
        rows = slice(row, row + 2 * C)
        gate = 0.0
        for j in range(m):
            gate += dot(gathered[j][rows, :], weight[rows_of(index[1] ^ j, width), :])
        gate_out[rows, :] = gate
        grad = upstream[rows, :].astype(F32) * (gate * jax.nn.sigmoid(gate))
        held[pair % 2] = grad.reshape(2, C, width)
        count = len(pieces) // BACK_HALVES
        for h in range(BACK_HALVES):
            columns = slice(h * width // BACK_HALVES, (h + 1) * width // BACK_HALVES)
            some = pieces[h * count : (h + 1) * count]
            scatter_rows(held.at[pair % 2], some, index[0], i, pair, columns)


def output_kernel(n, index, *refs):
    pieces, (gate_in, tokens, upstream, output, pre_grad, held) = refs[:-6], refs[-6:]
    for row, i, pair in blocks_of(output):
        rows = slice(row, row + 2 * C)
        for h in range(len(pieces) // n):
            some = pieces[h * n : (h + 1) * n]
            step = some[0].shape[-1]
            columns = slice(h * step, (h + 1) * step)
            gather_rows(held.at[pair % 2], some, index[0], i, pair, columns)
        mixed = held[pair % 2].reshape(2 * C, -1)
        gate = gate_in[rows, :]
        sig = jax.nn.sigmoid(gate)
        output[rows, :] = (tokens[rows, :].astype(F32) + mixed * (gate * sig)).astype(BF16)
        pre_grad[rows, :] = (
            upstream[rows, :].astype(F32) * mixed * sig * (1.0 + gate * (1.0 - sig))
        ).astype(BF16)


def split_dot(values, selector):
    top = values.astype(BF16)
    rest = values - top.astype(F32)
    middle = rest.astype(BF16)
    low = (rest - middle.astype(F32)).astype(BF16)
    return dot(top, selector) + dot(middle, selector) + dot(low, selector)


def back_kernel(n, own_a, index, *refs):
    grads, (second_big, third_big, back_second), pieces = refs[:n], refs[n : n + 3], refs[n + 3 :]
    for pair in range(B // 2):
        block = jnp.concatenate([g[:, pair].reshape(own_a * 2 * PER, -1) for g in grads], 0)
        back = dot(third_big[...], block).astype(BF16)
        back_second[:, pair] = back.reshape(A, 2 * PER, -1)
    for j in range(n):
        for i in range(own_a):
            block = back_second[j * own_a + i].reshape(B * PER, -1)
            pieces[j][i] = dot(second_big[...], block).astype(BF16).reshape(pieces[j].shape[1:])


def far_grad_kernel(n, own_a, index, *refs):
    cuts = [BACK_HALVES * n, HALVES * n, HALVES, BACK_HALVES]
    ends = [sum(cuts[: k + 1]) for k in range(4)]
    grads, first = refs[: ends[0]], refs[ends[0] : ends[1]]
    second_vals, back_vals = refs[ends[1] : ends[2]], refs[ends[2] : ends[3]]
    sums, third_acc, second_acc = refs[ends[3] :]
    big = 2 * A * PER
    small = B * PER

    def wide(blocks):
        return blocks[0] if len(blocks) == 1 else jnp.concatenate(blocks, 1)

    for pair in range(B // 2):
        sides = []
        for h in range(BACK_HALVES):
            some = grads[h * n : (h + 1) * n]
            sides.append(
                jnp.concatenate([g[:, pair].reshape(own_a * 2 * PER, -1) for g in some], 0)
            )
        other = wide([v[:, pair].reshape(big, -1) for v in second_vals])
        part = dot(wide(sides), other, ((1,), (1,)))
        third_acc[...] = part if pair == 0 else third_acc[...] + part
    for j in range(n):
        for i in range(own_a):
            block = wide([v[j * own_a + i].reshape(small, -1) for v in back_vals])
            other = wide([first[h * n + j][i].reshape(small, -1) for h in range(HALVES)])
            part = dot(block, other, ((1,), (1,)))
            second_acc[...] = part if j + i == 0 else second_acc[...] + part
    tall = own_a * 2 * PER
    row = lax.broadcasted_iota(jnp.int32, (tall, big), 0)
    col = lax.broadcasted_iota(jnp.int32, (tall, big), 1)
    keep = row % (2 * PER) == col % (2 * PER)
    source = lax.broadcasted_iota(jnp.int32, (big, 128), 0) // (2 * PER)
    source = ((source // own_a) ^ index[0]) * own_a + source % own_a
    lane = lax.broadcasted_iota(jnp.int32, (big, 128), 1)
    selector = (lane == source).astype(BF16)
    for block in range(n):
        picked = jnp.where(keep, third_acc[rows_of(index[0] ^ block, tall), :], 0.0)
        found = split_dot(picked, selector)
        total = found[: 2 * PER]
        for i in range(1, own_a):
            total += pltpu.roll(found[i * 2 * PER : (i + 1) * 2 * PER], i * A, 1)
        sums[block * PER : (block + 1) * PER, :] = total[:PER] + total[PER:]
    row = lax.broadcasted_iota(jnp.int32, (2 * PER, small), 0)
    col = lax.broadcasted_iota(jnp.int32, (2 * PER, small), 1)
    keep = row % PER == col % PER
    expand = lax.broadcasted_iota(jnp.int32, (small, 128), 0) // PER
    lane = lax.broadcasted_iota(jnp.int32, (small, 128), 1)
    total = 0.0
    for g in range(small // (2 * PER)):
        picked = jnp.where(keep, second_acc[g * 2 * PER : (g + 1) * 2 * PER, :], 0.0)
        total += split_dot(picked, (lane == expand + g * B).astype(BF16))
    sums[n * PER :, :] = total


def gate_grad_kernel(m, index, *refs):
    gathered, pre_grad, out = refs[:m], refs[m], refs[m + 1]
    width = pre_grad.shape[1]

    @pl.when(pl.program_id(0) == 0)
    def _():
        out[...] = jnp.zeros_like(out)

    for j in range(m):
        out[rows_of(index[1] ^ j, width), :] += dot(
            gathered[j][...], pre_grad[...], ((0,), (0,))
        )


def gate_input_kernel(m, index, *refs):
    grads, weights, upstream, out = refs[:m], refs[m : 2 * m], refs[2 * m], refs[2 * m + 1]
    total = upstream[...].astype(F32)
    for j in range(m):
        total += dot(grads[j][...], weights[j][...], ((1,), (1,)))
    out[...] = total


def first_grad_kernel(n, last, index, *refs):
    pieces, (tokens, *other, out, held, total) = refs[: n // 2], refs[n // 2 :]
    me = index[0]
    slots = range(n // 2, n) if last else range(n // 2)

    @pl.when(pl.program_id(0) == 0)
    def _():
        total[...] = jnp.zeros_like(total)

    for row, i, pair in blocks_of(tokens):
        for piece, j in zip(pieces, slots):
            place = rows_of((me ^ j) % (n // 2), PER)
            both = piece[i, pair].astype(F32)
            held[pair % 2, 0, place, :] = both[:PER]
            held[pair % 2, 1, place, :] = both[PER:]
        sides = []
        for side in range(2):
            rows = slice(row + side * C, row + (side + 1) * C)
            value = held[pair % 2, side].astype(BF16)
            sides.append(dot(value, tokens[rows, :], ((1,), (1,))))
        total[:, pair] += jnp.concatenate(sides, 1).reshape(n // 2, PER, 2 * C)

    @pl.when(pl.program_id(0) == pl.num_programs(0) - 1)
    def _():
        count = out.shape[0] // 2 if last else out.shape[0]
        mine = total[...].reshape(count, -1, 2 * C).astype(out.dtype)
        if last:
            half = me // (n // 2)
            out[pl.ds(half * count, count)] = other[0][...]
            out[pl.ds((1 - half) * count, count)] = mine
        else:
            out[...] = mine


def input_grad_kernel(n, index, *refs):
    pieces, (factor, partial, out, held) = refs[:n], refs[n:]
    for row, i, pair in blocks_of(out):
        gather_rows(held.at[pair % 2], pieces, index[0], i, pair)
        for side in range(2):
            rows = slice(row + side * C, row + (side + 1) * C)
            value = held[pair % 2, side].astype(BF16)
            mixed = dot(factor[2 * pair + side], value, ((0,), (0,)))
            out[rows, :] = (partial[rows, :] + mixed).astype(BF16)


def one_hot(dims, test):
    return test(
        lax.broadcasted_iota(jnp.int32, dims, 0), lax.broadcasted_iota(jnp.int32, dims, 1)
    ).astype(BF16)


def spread_kernel(own_a, back, index, third, second, third_big, second_big):
    me = index[0]

    def place(slot):
        return ((slot // own_a) ^ me) * own_a + slot % own_a

    def fill(values, copies, count, big, where):
        fast = copies * PER
        size = count * fast
        rows = one_hot(
            (size, PER * count), lambda r, k: k == (r % PER) * count + where(r // fast)
        )
        columns = one_hot((size, count), lambda r, k: k == where(r // fast))
        if back:
            picked = dot(columns, values, ((1,), (1,))).astype(BF16)
            wide = dot(picked, rows, ((1,), (1,)))
        else:
            picked = dot(rows, values).astype(BF16)
            wide = dot(picked, columns, ((1,), (1,)))
        row = lax.broadcasted_iota(jnp.int32, (size, size), 0)
        col = lax.broadcasted_iota(jnp.int32, (size, size), 1)
        big[...] = jnp.where(row % fast == col % fast, wide, 0.0).astype(BF16)

    own = third[pl.ds(pl.multiple_of(me * PER, PER), PER)].reshape(PER * A, A)
    fill(own, 2, A, third_big, place)
    own = second[pl.ds(pl.multiple_of(me * PER, PER), PER)].reshape(PER * B, B)
    fill(own, 1, B, second_big, lambda slot: slot)


def resident(tokens, cotangent, first_factor, second_factor, third_factor, gate_weight):
    n = lax.axis_size("seq")
    s = lax.axis_index("seq")
    m = lax.axis_size("ch")
    q = lax.axis_index("ch")
    rows, width = tokens.shape
    own_a = rows // (B * C)
    index = jnp.stack([s, q]).astype(jnp.int32)
    row_blocks = by_row(tokens, STEPS)
    pair_rows = pltpu.VMEM((2, 2, C, width), F32)

    far_tokens = swap(tokens, "ch", 2)
    half_width = width // HALVES
    half = shape((own_a, B // 2, 2 * PER, half_width), BF16)
    half_rows = [by_row(half, STEPS)] * n
    part_width = width // BACK_HALVES
    part = shape((own_a, B // 2, 2 * PER, part_width), BF16)
    part_rows = [by_row(part, STEPS)] * n
    far_part = shape((A, B // 2, 2 * PER, part_width), BF16)
    first_far = []
    for h in range(HALVES):
        columns = pl.BlockSpec((rows // STEPS, half_width), lambda i, *_, h=h: (i, h))
        sent = call(
            first_kernel, (STEPS,), index, (tokens, first_factor),
            [columns, whole(first_factor)], [half] * n, half_rows,
            [pltpu.VMEM((2, 2, C, half_width), F32)],
            2 * rows * half_width * C,
        )
        first_far.append(exchange(sent))
    gathered = [tokens, swap(tokens, "ch", 1), far_tokens, swap(far_tokens, "ch", 1)]
    weight_rows = [
        lax.dynamic_slice_in_dim(gate_weight, (q ^ j) * width, width, 0) for j in range(m)
    ]
    back_weight = [weight_rows[0]] + [swap(weight_rows[j], "ch", j) for j in range(1, m)]

    spread = []
    for back in (False, True):
        ins = (third_factor, second_factor)
        outs = [shape((2 * A * PER,) * 2, BF16), shape((B * PER,) * 2, BF16)]
        spread += call(
            functools.partial(spread_kernel, own_a, back), (1,), index, ins,
            [whole(x) for x in ins], outs, [whole(x) for x in outs], (),
            0,
        )
    third_big, second_big, third_back, second_back = spread

    far_half = shape((A, B // 2, 2 * PER, half_width), BF16)
    second_far, mixed_home = [], []
    for h in range(HALVES):
        ins = (*first_far[h], second_big, third_big)
        outs = [far_half] + [half] * n
        second_val, *sent = call(
            functools.partial(far_kernel, n, own_a), (1,), index, ins,
            [whole(x) for x in ins], outs, [whole(x) for x in outs],
            (), 2 * rows * half_width * 6 * C,
        )
        second_far.append(second_val)
        mixed_home += exchange(sent)

    gate_shape = shape((rows, width), F32)
    ins = (*gathered, gate_weight, cotangent)
    gate_pre, *sent = call(
        functools.partial(gate_kernel, m), (STEPS,), index, ins,
        [row_blocks] * m + [whole(gate_weight), row_blocks],
        [gate_shape] + [part] * (n * BACK_HALVES),
        [row_blocks] + part_rows * BACK_HALVES, [pair_rows],
        2 * rows * width * m * width,
    )
    grad_far = [exchange(sent[h * n : (h + 1) * n]) for h in range(BACK_HALVES)]

    ins = (*mixed_home, gate_pre, tokens, cotangent)
    output, pre_grad = call(
        functools.partial(output_kernel, n), (STEPS,), index, ins,
        half_rows * HALVES + [row_blocks] * 3,
        [shape((rows, width), BF16)] * 2, [row_blocks] * 2,
        [pair_rows], rows * width * 16,
    )
    far_pre = swap(pre_grad, "ch", 2)
    all_pre = [pre_grad, swap(pre_grad, "ch", 1), far_pre, swap(far_pre, "ch", 1)]

    back_home, back_far = [], []
    for h in range(BACK_HALVES):
        ins = (*grad_far[h], second_back, third_back)
        outs = [far_part] + [part] * n
        back_second, *sent = call(
            functools.partial(back_kernel, n, own_a), (1,), index, ins,
            [whole(x) for x in ins], outs, [whole(x) for x in outs], (),
            2 * rows * part_width * 6 * C,
        )
        back_far.append(back_second)
        back_home.append(exchange(sent))

    def flat(halves):
        return [x for half_pieces in halves for x in half_pieces]

    ins = (*flat(grad_far), *flat(first_far), *second_far, *back_far)
    outs = [shape((n * PER + 2 * PER, 128), F32)]
    sums = call(
        functools.partial(far_grad_kernel, n, own_a), (1,), index, ins,
        [whole(x) for x in ins], outs, [whole(x) for x in outs],
        [
            pltpu.VMEM((2 * A * PER, 2 * A * PER), F32),
            pltpu.VMEM((B * PER, B * PER), F32),
        ],
        2 * rows * width * 10 * C,
    )[0]

    out = shape((m * width, width), F32)
    gate_part = call(
        functools.partial(gate_grad_kernel, m), (STEPS,), index, (*gathered, pre_grad),
        [row_blocks] * (m + 1), [out], [whole(out)], (),
        2 * rows * width * m * width,
    )[0].reshape(n, m * width // n, width)
    bit = 1
    while bit < n:
        mine = (s // bit) % 2
        split = gate_part.reshape(n // (2 * bit), 2, *gate_part.shape[1:])
        keep = lax.dynamic_index_in_dim(split, mine, 1, False)
        send = lax.dynamic_index_in_dim(split, 1 - mine, 1, False)
        gate_part = keep + swap(send, "seq", bit)
        bit *= 2
    gate_grad = gate_part.reshape(m * width // n, width)

    ins = (*all_pre, *back_weight, cotangent)
    partial = call(
        functools.partial(gate_input_kernel, m), (STEPS,), index, ins,
        [row_blocks] * m + [whole(w) for w in back_weight] + [row_blocks],
        [gate_shape], [row_blocks], (), 2 * rows * width * m * width,
    )[0]

    bit = m // 2
    while bit:
        sums = sums + swap(sums, "ch", bit)
        bit //= 2
    every = jnp.broadcast_to(sums.astype(BF16)[None], (n, *sums.shape))
    every = lax.all_to_all(every, "seq", split_axis=0, concat_axis=0, tiled=True)
    third_all = every[:, : n * PER].reshape(n, n, PER, 128).transpose(0, 2, 1, 3)
    third_grad = third_all.reshape(C, A, A)
    second_all = every[:, n * PER :].reshape(n, 2, PER, B // 2, B)
    second_grad = second_all.transpose(0, 2, 3, 1, 4).reshape(C, B, B)

    first_out = shape((n * m, B * C // (2 * n * m), 2 * C), BF16)
    near_out = shape((n * m // 2, *first_out.shape[1:]), BF16)
    home = back_home[0]
    held_half = pltpu.VMEM((2, 2, n // 2 * PER, width), F32)
    total_half = pltpu.VMEM((n // 2, B // 2, PER, 2 * C), F32)
    parts = ()
    for last in (False, True):
        ins = (*(home[n // 2 :] if last else home[: n // 2]), tokens, *parts)
        outs = [first_out if last else near_out]
        parts = call(
            functools.partial(first_grad_kernel, n, last), (STEPS,), index, ins,
            part_rows[: n // 2] + [row_blocks] + [whole(x) for x in parts],
            outs, [whole(outs[0])], [held_half, total_half],
            rows * width * C,
        )
    parts = parts[0]
    parts = lax.all_to_all(parts, ("seq", "ch"), split_axis=0, concat_axis=0, tiled=True)
    first_sum = parts.astype(F32).sum(0).astype(BF16)
    first_sum = lax.all_to_all(
        jnp.broadcast_to(first_sum[None], (n * m, *first_sum.shape)),
        ("seq", "ch"), split_axis=0, concat_axis=0, tiled=True,
    )
    first_grad = first_sum.reshape(n, B // 2, PER, 2, C).transpose(1, 3, 0, 2, 4)
    first_grad = first_grad.reshape(B, C, C)

    ins = (*home, first_factor, partial)
    input_grad = call(
        functools.partial(input_grad_kernel, n), (STEPS,), index, ins,
        part_rows + [whole(first_factor), row_blocks],
        [shape((rows, width), BF16)], [row_blocks], [pair_rows], 2 * rows * width * C,
    )[0]
    return output, input_grad, first_grad, second_grad, third_grad, gate_grad


def spread_out(tokens, cotangent, first_factor, second_factor, third_factor, gate_weight):
    seq_count = lax.axis_size("seq")
    seq_index = lax.axis_index("seq")
    per_device_c = max(1, C // seq_count)
    splits = max(1, seq_count // C)
    local_rows, width = tokens.shape
    narrow = width // splits
    blocks = local_rows // C
    batch_b = min(blocks, B)
    start_b = seq_index * blocks % B
    if blocks >= B:
        first_sel = first_factor
    else:
        first_sel = lax.dynamic_slice_in_dim(first_factor, start_b, blocks, 0)
    column = seq_index // splits * per_device_c
    second_sel = lax.dynamic_slice_in_dim(second_factor, column, per_device_c, 0)
    third_sel = lax.dynamic_slice_in_dim(third_factor, column, per_device_c, 0)
    grid_view = tokens.reshape(blocks // batch_b, batch_b, C, width)
    mixed_first = jnp.einsum(
        "bcd,ibdh->ibch", first_sel, grid_view, preferred_element_type=jnp.float32
    ).astype(jnp.bfloat16)

    def spread(values):
        return values.reshape(blocks, seq_count, per_device_c, narrow)

    received = lax.all_to_all(spread(mixed_first), "seq", split_axis=1, concat_axis=0, tiled=True)
    item_count = received.shape[3]
    far_view = received.reshape(A, B, per_device_c, item_count)
    second_val = jnp.einsum(
        "kbe,aekh->abkh", second_sel, far_view, preferred_element_type=jnp.float32
    ).astype(jnp.bfloat16)
    third_val = jnp.einsum(
        "kae,ebkh->abkh", third_sel, second_val, preferred_element_type=jnp.float32
    ).astype(jnp.bfloat16)
    first_far = received
    second_far = second_val.reshape(A * B, 1, per_device_c, item_count)
    mixed_far = third_val.reshape(A * B, 1, per_device_c, item_count)
    mixed_back = lax.all_to_all(mixed_far, "seq", split_axis=0, concat_axis=1, tiled=True).reshape(
        local_rows, width
    )
    full_tokens, full_weight = (
        lax.all_gather(tokens, "ch", axis=1, tiled=True),
        lax.all_gather(gate_weight, "ch", axis=1, tiled=True),
    )
    own_rows = lax.dynamic_slice_in_dim(full_weight, lax.axis_index("ch") * width, width, 0)
    gate_pre = jnp.dot(full_tokens, gate_weight, preferred_element_type=jnp.float32)
    sigmoid_gate = jax.nn.sigmoid(gate_pre)
    activation = gate_pre * sigmoid_gate
    mixed_float = mixed_back.astype(jnp.float32)
    output = (tokens.astype(jnp.float32) + mixed_float * activation).astype(jnp.bfloat16)
    upstream = cotangent.astype(jnp.float32)
    mix_grad = (upstream * activation).astype(jnp.bfloat16)
    pre_grad = (
        upstream * mixed_float * sigmoid_gate * (1.0 + gate_pre * (1.0 - sigmoid_gate))
    ).astype(jnp.bfloat16)
    received = lax.all_to_all(spread(mix_grad), "seq", split_axis=1, concat_axis=0, tiled=True)
    item_count = received.shape[3]
    far_view = received.reshape(A, B, per_device_c, item_count)
    back_second = jnp.einsum(
        "kae,abkh->ebkh", third_sel, far_view, preferred_element_type=jnp.float32
    ).astype(jnp.bfloat16)
    back_first = jnp.einsum(
        "kbe,abkh->aekh", second_sel, back_second, preferred_element_type=jnp.float32
    ).astype(jnp.bfloat16)
    second_back = back_second.reshape(A * B, 1, per_device_c, item_count)
    first_back = back_first.reshape(A * B, 1, per_device_c, item_count)
    third_part = jnp.einsum(
        "abkh,ebkh->kae",
        received.reshape(A, B, per_device_c, narrow),
        second_far.reshape(A, B, per_device_c, narrow),
        preferred_element_type=jnp.float32,
    )
    second_part = jnp.einsum(
        "abkh,aekh->kbe",
        second_back.reshape(A, B, per_device_c, narrow),
        first_far.reshape(A, B, per_device_c, narrow),
        preferred_element_type=jnp.float32,
    )
    first_home = lax.all_to_all(first_back, "seq", split_axis=0, concat_axis=1, tiled=True).reshape(
        blocks // batch_b, batch_b, C, width
    )
    mix_input = jnp.einsum(
        "bcd,ibch->ibdh", first_sel, first_home, preferred_element_type=jnp.float32
    ).reshape(local_rows, width)
    first_part = jnp.einsum(
        "ibch,ibdh->bcd", first_home, grid_view, preferred_element_type=jnp.float32
    )
    if blocks >= B:
        first_full = first_part
    else:
        first_full = lax.dynamic_update_slice_in_dim(
            jnp.zeros((B, C, C), jnp.float32), first_part, start_b, 0
        )
    second_full = lax.dynamic_update_slice_in_dim(
        jnp.zeros((C, B, B), jnp.float32), second_part, column, 0
    )
    third_full = lax.dynamic_update_slice_in_dim(
        jnp.zeros((C, A, A), jnp.float32), third_part, column, 0
    )
    first_sum, second_sum, third_sum = lax.psum(
        (first_full, second_full, third_full), ("seq", "ch")
    )
    gate_input = lax.dot_general(
        lax.all_gather(pre_grad, "ch", axis=1, tiled=True),
        own_rows,
        (((1,), (1,)), ((), ())),
        preferred_element_type=jnp.float32,
    )
    gate_grad = lax.psum_scatter(
        lax.dot_general(
            full_tokens, pre_grad, (((0,), (0,)), ((), ())), preferred_element_type=jnp.float32
        ),
        "seq",
        scatter_dimension=0,
        tiled=True,
    )
    input_grad = (upstream + mix_input + gate_input).astype(jnp.bfloat16)
    return (
        output,
        input_grad,
        first_sum.astype(jnp.bfloat16),
        second_sum.astype(jnp.bfloat16),
        third_sum.astype(jnp.bfloat16),
        gate_grad,
    )


def on_device(*arrays):
    n = lax.axis_size("seq")
    rows = arrays[0].shape[0]
    square = lax.axis_size("ch") == 4 and n * PER == C
    if square and rows % (B * C) == 0 and rows * n == A * B * C:
        return resident(*arrays)
    return spread_out(*arrays)


def solution(mesh):
    placed = (P("seq", "ch"), P("seq", "ch"), P(), P(), P(), P(None, "ch"))
    return jax.shard_map(
        on_device,
        mesh=mesh,
        in_specs=placed,
        out_specs=(P("seq", "ch"), P("seq", "ch"), P(), P(), P(), P("seq", "ch")),
        check_vma=False,
    )
```
